32 devices in a mesh: space: 2 (over x), vel: 16 (over z, y, core).
Axes of the slice: x: 2, y: 2, z: 4, core: 2. Of those that a mesh axis runs over, the one named last changes fastest.
Arguments:
- distribution: float32 [8192, 512], P('vel', 'space'), may hold values from 0.1 to 32, as said below
- normals: float32 [4, 3, 512], P(None, None, 'space'), may hold values from -0.3 to 0.3
- adjacency: int32 [4, 512], P(None, 'space'), may hold values from 0 to 511, as said below
- send_list: int32 [2, 2, 256], P('space'), may hold values from 0 to 255
- block_counts: int32 [2, 2], P(None, 'space'), may hold values from 0 to 2, as said below
Outputs:
- relaxed: float32 [8192, 512], P('vel', 'space')
- fields: float32 [13, 512], P(None, 'space')
The draws below stay inside these ranges and needn't reach their ends.
Inputs may be any that keep to these rules, and one draw needn't show every extreme that they name: `adjacency`: every entry of 256 or more names a position below 128 times the sum of block_counts over the senders to its group. `block_counts`: no group sends to itself; every other pair has at least one block; one receiving group gets 2 blocks from every other group. `distribution`: Positive.
All inputs are finite; a program needn't handle non-finite values.
Results may differ from the reference program's by a relative error of at most 0.00011.
Values sent between devices are 32-bit elements; how exact they have to be, the bound alone decides.
A program may use at most 64 MiB of HBM per device.

```python
import math
import jax
import jax.numpy as jnp
from jax import lax

VXY = 32
C_DEV = 256
FACES = 4
TILE = 128
MAXB = 2
BND = 256
ITERS = 2
V = 8192
VZN = 8
CELLS = 512
SLOTS = 256
N_SPACE = 2


def counts_core(key):
    key_one, key_three = jax.random.split(jax.random.fold_in(key, 11), 2)
    counts = jax.random.randint(key_one, (N_SPACE, N_SPACE), 1, MAXB + 1)
    full_group = jax.random.randint(key_three, (), 0, N_SPACE)
    row_ids = jnp.arange(N_SPACE)[:, None]
    col_ids = jnp.arange(N_SPACE)[None, :]
    counts = jnp.where(col_ids == full_group, MAXB, counts)
    return (jnp.where(row_ids == col_ids, 0, counts).astype(jnp.int32), full_group)


def draw_block_counts(key, part):
    counts, full_group = counts_core(key)
    return counts


def draw_adjacency(key, part):
    counts, full_group = counts_core(key)
    packed_total = jnp.sum(counts, axis=0) * TILE
    key_a, key_b, key_c = jax.random.split(jax.random.fold_in(key, 23), 3)
    group_of = jnp.arange(C_DEV * N_SPACE) // C_DEV
    limit = packed_total[group_of]
    local_pick = jax.random.randint(key_a, (FACES, C_DEV * N_SPACE), 0, C_DEV)
    ghost_pick = jax.random.randint(key_b, (FACES, C_DEV * N_SPACE), 0, 1 << 20) % limit[None, :]
    remote = jax.random.randint(key_c, (FACES, C_DEV * N_SPACE), 0, 8) == 0
    result = jnp.where(remote, C_DEV + ghost_pick, local_pick)
    first_cell = full_group * C_DEV
    face_ids = jnp.arange(FACES)[:, None]
    cell_ids = jnp.arange(C_DEV * N_SPACE)[None, :]
    top_value = C_DEV + (N_SPACE - 1) * SLOTS - 1
    result = jnp.where((face_ids == 0) & (cell_ids == first_cell), top_value, result)
    result = jnp.where((face_ids == 1) & (cell_ids == first_cell), 0, result)
    return result.astype(jnp.int32)


def draw_distribution(key, part):
    level = (jnp.arange(V) // (VXY * VXY)).astype(jnp.float32)
    comp_z = (level - (VZN - 1) / 2.0) * 0.3
    z_span = max(VZN - 1, 1) * 0.3
    key_one = jax.random.fold_in(key, 0)
    rough = jnp.exp(jax.random.uniform(key_one, (V, C_DEV * N_SPACE), jnp.float32, math.log(0.3), math.log(3.0)))
    tilt = math.log(5.0) / z_span
    return (rough * jnp.exp(tilt * comp_z)[:, None]).astype(jnp.float32)


def plant(values, own_key, smallest, largest):
    longest = values.shape.index(max(values.shape))
    spots = []
    for shift in (0, 1):
        where = [jax.random.randint(jax.random.fold_in(own_key, axis), (), 0, length) for axis, length in enumerate(values.shape)]
        where[longest] = (where[longest] + shift) % values.shape[longest]
        spots.append(tuple(where))
    return values.at[spots[0]].set(smallest).at[spots[1]].set(largest)


def block_levels(own_key, shape, cuts, least, largest):
    def one(dim, shards_of):
        heights = jax.random.uniform(jax.random.fold_in(jax.random.fold_in(own_key, 6), dim), (shards_of,), jnp.float32, least / len(cuts), largest / len(cuts))
        return jnp.repeat(jnp.exp(heights), shape[dim] // shards_of).reshape((-1,) + (1,) * (len(shape) - dim - 1))

    factor_of = one(*cuts[0])
    for cut in cuts[1:]:
        factor_of = factor_of * one(*cut)
    return factor_of


def setup_inputs(seed: int = 0) -> dict:
    key_list = jax.random.split(jax.random.key(seed), 6)
    distribution = draw_distribution(jax.random.fold_in(key_list[5], 71), 0)
    normals = jnp.clip(jax.random.uniform(key_list[1], (FACES, 3, CELLS), jnp.float32, -0.3, 0.3) * block_levels(key_list[1], (FACES, 3, CELLS), ((2, 2),), -0.4, 0.0), -0.3, 0.3)
    adjacency = draw_adjacency(jax.random.fold_in(key_list[5], 71), 0)
    send_list = plant(jax.random.randint(key_list[3], (N_SPACE, N_SPACE, SLOTS), 0, BND), jax.random.fold_in(key_list[3], 1), 0, BND - 1).astype(jnp.int32)
    block_counts = draw_block_counts(jax.random.fold_in(key_list[5], 71), 0)
    return {"distribution": distribution, "normals": normals, "adjacency": adjacency, "send_list": send_list, "block_counts": block_counts}


spacing = 0.3
ellipsoid_mix = -0.25
prandtl = 0.8
visc_power = 0.26
time_step = 0.025


def velocity_nodes(vel_index, z_count):
    comp_x = (vel_index % VXY).astype(jnp.float32)
    comp_y = ((vel_index // VXY) % VXY).astype(jnp.float32)
    comp_z = (vel_index // (VXY * VXY)).astype(jnp.float32)
    centre = (VXY - 1) / 2.0
    return jnp.stack([(comp_x - centre) * spacing, (comp_y - centre) * spacing, (comp_z - (z_count - 1) / 2.0) * spacing])


def moment_rows(velocity):
    comp_x, comp_y, comp_z = velocity[0], velocity[1], velocity[2]
    squared = comp_x * comp_x + comp_y * comp_y + comp_z * comp_z
    return jnp.stack([jnp.ones_like(comp_x), comp_x, comp_y, comp_z, comp_x * comp_x, comp_y * comp_y, comp_z * comp_z, comp_x * comp_y, comp_x * comp_z, comp_y * comp_z, comp_x * squared, comp_y * squared, comp_z * squared])


def quad_rows(velocity):
    comp_x, comp_y, comp_z = velocity[0], velocity[1], velocity[2]
    return jnp.stack([comp_x * comp_x, comp_y * comp_y, comp_z * comp_z, comp_x * comp_y, comp_x * comp_z, comp_y * comp_z, comp_x, comp_y, comp_z, jnp.ones_like(comp_x)])


def macroscopic(moments):
    density = moments[0]
    mean_x = moments[1] / density
    mean_y = moments[2] / density
    mean_z = moments[3] / density
    second = moments[4:10] / density[None, :]
    third = moments[10:13] / density[None, :]
    theta_xx = second[0] - mean_x * mean_x
    theta_yy = second[1] - mean_y * mean_y
    theta_zz = second[2] - mean_z * mean_z
    theta_xy = second[3] - mean_x * mean_y
    theta_xz = second[4] - mean_x * mean_z
    theta_yz = second[5] - mean_y * mean_z
    temper = (theta_xx + theta_yy + theta_zz) / 3.0
    trace_b = second[0] + second[1] + second[2]
    bu_x = second[0] * mean_x + second[3] * mean_y + second[4] * mean_z
    bu_y = second[3] * mean_x + second[1] * mean_y + second[5] * mean_z
    bu_z = second[4] * mean_x + second[5] * mean_y + second[2] * mean_z
    mean_sq = mean_x * mean_x + mean_y * mean_y + mean_z * mean_z
    flux_x = 0.5 * (third[0] - 2.0 * bu_x - mean_x * trace_b + 2.0 * mean_x * mean_sq)
    flux_y = 0.5 * (third[1] - 2.0 * bu_y - mean_y * trace_b + 2.0 * mean_y * mean_sq)
    flux_z = 0.5 * (third[2] - 2.0 * bu_z - mean_z * trace_b + 2.0 * mean_z * mean_sq)
    iso_part = (1.0 - ellipsoid_mix) * temper
    lam_xx = iso_part + ellipsoid_mix * theta_xx
    lam_yy = iso_part + ellipsoid_mix * theta_yy
    lam_zz = iso_part + ellipsoid_mix * theta_zz
    lam_xy = ellipsoid_mix * theta_xy
    lam_xz = ellipsoid_mix * theta_xz
    lam_yz = ellipsoid_mix * theta_yz
    cof_xx = lam_yy * lam_zz - lam_yz * lam_yz
    cof_xy = lam_yz * lam_xz - lam_xy * lam_zz
    cof_xz = lam_xy * lam_yz - lam_yy * lam_xz
    cof_yy = lam_xx * lam_zz - lam_xz * lam_xz
    cof_yz = lam_xy * lam_xz - lam_xx * lam_yz
    cof_zz = lam_xx * lam_yy - lam_xy * lam_xy
    determinant = lam_xx * cof_xx + lam_xy * cof_xy + lam_xz * cof_xz
    inv_xx = cof_xx / determinant
    inv_yy = cof_yy / determinant
    inv_zz = cof_zz / determinant
    inv_xy = cof_xy / determinant
    inv_xz = cof_xz / determinant
    inv_yz = cof_yz / determinant
    lin_x = inv_xx * mean_x + inv_xy * mean_y + inv_xz * mean_z
    lin_y = inv_xy * mean_x + inv_yy * mean_y + inv_yz * mean_z
    lin_z = inv_xz * mean_x + inv_yz * mean_y + inv_zz * mean_z
    offset = mean_x * lin_x + mean_y * lin_y + mean_z * lin_z
    collide = prandtl * density * jnp.exp(visc_power * jnp.log(temper))
    return jnp.stack([density, mean_x, mean_y, mean_z, theta_xx, theta_yy, theta_zz, theta_xy, theta_xz, theta_yz, flux_x, flux_y, flux_z,
                      inv_xx, inv_yy, inv_zz, 2.0 * inv_xy, 2.0 * inv_xz, 2.0 * inv_yz, -2.0 * lin_x, -2.0 * lin_y, -2.0 * lin_z, offset, collide])


def ghost_slots(adjacency, counts, cells, groups, slot_count):
    ends = (jnp.cumsum(counts) * TILE).astype(jnp.int32)
    starts = (ends - counts * TILE).astype(jnp.int32)
    is_local = adjacency < cells
    position = jnp.maximum(adjacency - cells, 0)
    source = jnp.sum((ends[:, None, None] <= position[None]).astype(jnp.int32), axis=0).astype(jnp.int32)
    source = jnp.minimum(source, groups - 1)
    group_ids = jnp.arange(groups, dtype=jnp.int32)[:, None, None]
    chosen = jnp.sum(jnp.where(group_ids == source[None], starts[:, None, None], 0), axis=0).astype(jnp.int32)
    slot_pos = jnp.clip(position - chosen, 0, slot_count - 1).astype(jnp.int32)
    return is_local, source, slot_pos


def relax(current, neighbours, velocity, normals, params, norm_z, equilibrium):
    gauss = params[0][None, :] * equilibrium / norm_z[None, :]
    outflow = jnp.zeros(current.shape, jnp.float32)
    inflow = jnp.zeros(current.shape, jnp.float32)
    for side in range(normals.shape[0]):
        normal_speed = (velocity[0][:, None] * normals[side, 0][None, :] + velocity[1][:, None] * normals[side, 1][None, :]
                        + velocity[2][:, None] * normals[side, 2][None, :])
        outflow = outflow + jnp.maximum(normal_speed, 0.0)
        inflow = inflow + jnp.minimum(normal_speed, 0.0) * neighbours[side]
    return current + time_step * (params[23][None, :] * (gauss - current) - outflow * current - inflow)


def reference(distribution, normals, adjacency, send_list, block_counts):
    pieces = []
    for group in range(N_SPACE):
        local_adj = adjacency[:, group * C_DEV:(group + 1) * C_DEV]
        is_local, source, slot_pos = ghost_slots(local_adj, block_counts[:, group], C_DEV, N_SPACE, SLOTS)
        listed = send_list[:, group, :]
        remote = source * C_DEV + listed[source, slot_pos]
        pieces.append(jnp.where(is_local, group * C_DEV + local_adj, remote).astype(jnp.int32))
    neighbour_index = jnp.concatenate(pieces, axis=1)
    level_count = V // (VXY * VXY)
    block_rows = VXY * VXY
    velocity = velocity_nodes(jnp.arange(V, dtype=jnp.int32), level_count)
    moment_table = moment_rows(velocity)
    quad_table = quad_rows(velocity).T
    vel_blocks = velocity.reshape(3, level_count, block_rows).transpose(1, 0, 2)
    quad_blocks = quad_table.reshape(level_count, block_rows, 10)

    def reduce_moments(current):
        partial_value = jnp.dot(moment_table, current, precision=lax.Precision.HIGHEST, preferred_element_type=jnp.float32)
        return macroscopic(partial_value / V)

    current = distribution
    for iteration in range(ITERS):
        params = reduce_moments(current)

        def block_equilibrium(quad_block):
            exponent = jnp.dot(quad_block, params[13:23], precision=lax.Precision.HIGHEST, preferred_element_type=jnp.float32)
            return jnp.exp(-0.5 * exponent)

        norm_z = jnp.sum(lax.map(lambda quad_block: jnp.sum(block_equilibrium(quad_block), axis=0), quad_blocks), axis=0) / V
        state_blocks = current.reshape(level_count, block_rows, CELLS)

        def update(inputs):
            state_block, vel_block, quad_block = inputs
            neighbours = [jnp.take(state_block, neighbour_index[side], axis=1) for side in range(FACES)]
            return relax(state_block, neighbours, vel_block, normals, params, norm_z, block_equilibrium(quad_block))

        current = lax.map(update, (state_blocks, vel_blocks, quad_blocks)).reshape(V, CELLS)
    final = reduce_moments(current)
    return current, final[:13]
```

```python
import functools

import jax
import jax.numpy as jnp
from jax import lax
from jax.experimental import pallas as pl
from jax.experimental.pallas import tpu as pltpu
from jax.sharding import PartitionSpec as P

VXY = 32
TILE = 128
ITERS = 2


spacing = 0.3
ellipsoid_mix = -0.25
prandtl = 0.8
visc_power = 0.26
time_step = 0.025


def velocity_nodes(vel_index, z_count):
    comp_x = (vel_index % VXY).astype(jnp.float32)
    comp_y = (vel_index // VXY % VXY).astype(jnp.float32)
    comp_z = (vel_index // (VXY * VXY)).astype(jnp.float32)
    centre = (VXY - 1) / 2.0
    return jnp.stack(
        [
            (comp_x - centre) * spacing,
            (comp_y - centre) * spacing,
            (comp_z - (z_count - 1) / 2.0) * spacing,
        ]
    )


def moment_rows(velocity):
    comp_x, comp_y, comp_z = (velocity[0], velocity[1], velocity[2])
    squared = comp_x * comp_x + comp_y * comp_y + comp_z * comp_z
    return jnp.stack(
        [
            jnp.ones_like(comp_x),
            comp_x,
            comp_y,
            comp_z,
            comp_x * comp_x,
            comp_y * comp_y,
            comp_z * comp_z,
            comp_x * comp_y,
            comp_x * comp_z,
            comp_y * comp_z,
            comp_x * squared,
            comp_y * squared,
            comp_z * squared,
        ]
    )


def quad_rows(velocity):
    comp_x, comp_y, comp_z = (velocity[0], velocity[1], velocity[2])
    return jnp.stack(
        [
            comp_x * comp_x,
            comp_y * comp_y,
            comp_z * comp_z,
            comp_x * comp_y,
            comp_x * comp_z,
            comp_y * comp_z,
            comp_x,
            comp_y,
            comp_z,
            jnp.ones_like(comp_x),
        ]
    )


def macroscopic(moments):
    density = moments[0]
    mean_x = moments[1] / density
    mean_y = moments[2] / density
    mean_z = moments[3] / density
    second = moments[4:10] / density[None, :]
    third = moments[10:13] / density[None, :]
    theta_xx = second[0] - mean_x * mean_x
    theta_yy = second[1] - mean_y * mean_y
    theta_zz = second[2] - mean_z * mean_z
    theta_xy = second[3] - mean_x * mean_y
    theta_xz = second[4] - mean_x * mean_z
    theta_yz = second[5] - mean_y * mean_z
    temper = (theta_xx + theta_yy + theta_zz) / 3.0
    trace_b = second[0] + second[1] + second[2]
    bu_x = second[0] * mean_x + second[3] * mean_y + second[4] * mean_z
    bu_y = second[3] * mean_x + second[1] * mean_y + second[5] * mean_z
    bu_z = second[4] * mean_x + second[5] * mean_y + second[2] * mean_z
    mean_sq = mean_x * mean_x + mean_y * mean_y + mean_z * mean_z
    flux_x = 0.5 * (third[0] - 2.0 * bu_x - mean_x * trace_b + 2.0 * mean_x * mean_sq)
    flux_y = 0.5 * (third[1] - 2.0 * bu_y - mean_y * trace_b + 2.0 * mean_y * mean_sq)
    flux_z = 0.5 * (third[2] - 2.0 * bu_z - mean_z * trace_b + 2.0 * mean_z * mean_sq)
    iso_part = (1.0 - ellipsoid_mix) * temper
    lam_xx = iso_part + ellipsoid_mix * theta_xx
    lam_yy = iso_part + ellipsoid_mix * theta_yy
    lam_zz = iso_part + ellipsoid_mix * theta_zz
    lam_xy = ellipsoid_mix * theta_xy
    lam_xz = ellipsoid_mix * theta_xz
    lam_yz = ellipsoid_mix * theta_yz
    cof_xx = lam_yy * lam_zz - lam_yz * lam_yz
    cof_xy = lam_yz * lam_xz - lam_xy * lam_zz
    cof_xz = lam_xy * lam_yz - lam_yy * lam_xz
    cof_yy = lam_xx * lam_zz - lam_xz * lam_xz
    cof_yz = lam_xy * lam_xz - lam_xx * lam_yz
    cof_zz = lam_xx * lam_yy - lam_xy * lam_xy
    determinant = lam_xx * cof_xx + lam_xy * cof_xy + lam_xz * cof_xz
    inv_xx = cof_xx / determinant
    inv_yy = cof_yy / determinant
    inv_zz = cof_zz / determinant
    inv_xy = cof_xy / determinant
    inv_xz = cof_xz / determinant
    inv_yz = cof_yz / determinant
    lin_x = inv_xx * mean_x + inv_xy * mean_y + inv_xz * mean_z
    lin_y = inv_xy * mean_x + inv_yy * mean_y + inv_yz * mean_z
    lin_z = inv_xz * mean_x + inv_yz * mean_y + inv_zz * mean_z
    offset = mean_x * lin_x + mean_y * lin_y + mean_z * lin_z
    collide = prandtl * density * jnp.exp(visc_power * jnp.log(temper))
    return jnp.stack(
        [
            density,
            mean_x,
            mean_y,
            mean_z,
            theta_xx,
            theta_yy,
            theta_zz,
            theta_xy,
            theta_xz,
            theta_yz,
            flux_x,
            flux_y,
            flux_z,
            inv_xx,
            inv_yy,
            inv_zz,
            2.0 * inv_xy,
            2.0 * inv_xz,
            2.0 * inv_yz,
            -2.0 * lin_x,
            -2.0 * lin_y,
            -2.0 * lin_z,
            offset,
            collide,
        ]
    )


def ghost_slots(adjacency, counts, cells, groups, slot_count):
    ends = jnp.cumsum(counts) * TILE
    starts = ends - counts * TILE
    is_local = adjacency < cells
    position = jnp.maximum(adjacency - cells, 0)
    source = jnp.sum((ends[:, None, None] <= position[None]).astype(jnp.int32), axis=0)
    source = jnp.minimum(source, groups - 1)
    group_ids = jnp.arange(groups, dtype=jnp.int32)[:, None, None]
    chosen = jnp.sum(jnp.where(group_ids == source[None], starts[:, None, None], 0), axis=0)
    slot_pos = jnp.clip(position - chosen, 0, slot_count - 1)
    return (is_local, source, slot_pos)


def relax(current, neighbours, velocity, normals, params, norm_z, equilibrium):
    gauss = params[0][None, :] * equilibrium / norm_z[None, :]
    outflow = jnp.zeros(current.shape, jnp.float32)
    inflow = jnp.zeros(current.shape, jnp.float32)
    for side in range(normals.shape[0]):
        normal_speed = (
            velocity[0][:, None] * normals[side, 0][None, :]
            + velocity[1][:, None] * normals[side, 1][None, :]
            + velocity[2][:, None] * normals[side, 2][None, :]
        )
        outflow = outflow + jnp.maximum(normal_speed, 0.0)
        inflow = inflow + jnp.minimum(normal_speed, 0.0) * neighbours[side]
    return current + time_step * (
        params[23][None, :] * (gauss - current) - outflow * current - inflow
    )


def per_device(distribution, normals, adjacency, send_list, block_counts):
    vel_local = distribution.shape[0]
    cells = distribution.shape[1]
    total_vel = vel_local * lax.axis_size("vel")
    z_count = total_vel // (VXY * VXY)
    groups = send_list.shape[1]
    slot_count = send_list.shape[2]
    vel_index = lax.axis_index("vel") * vel_local + jnp.arange(vel_local, dtype=jnp.int32)
    velocity = velocity_nodes(vel_index, z_count)
    moment_table = moment_rows(velocity)
    quad_table = quad_rows(velocity).T
    is_local, source, slot_pos = ghost_slots(
        adjacency, block_counts[:, 0], cells, groups, slot_count
    )
    ghost_index = source * slot_count + slot_pos
    local_index = jnp.where(is_local, adjacency, 0)
    send_rows = send_list[0].reshape(-1)

    def reduce_moments(current):
        partial_value = (
            jnp.dot(
                moment_table,
                current,
                precision=lax.Precision.HIGHEST,
                preferred_element_type=jnp.float32,
            )
            / total_vel
        )
        return macroscopic(lax.psum(partial_value, "vel"))

    current = distribution
    for iteration in range(ITERS):
        params = reduce_moments(current)
        ghosts = lax.all_to_all(
            jnp.take(current, send_rows, axis=1), "space", split_axis=1, concat_axis=1, tiled=True
        )
        exponent = jnp.dot(
            quad_table,
            params[13:23],
            precision=lax.Precision.HIGHEST,
            preferred_element_type=jnp.float32,
        )
        equilibrium = jnp.exp(-0.5 * exponent)
        norm_z = lax.psum(jnp.sum(equilibrium, axis=0) / total_vel, "vel")
        neighbours = [
            jnp.where(
                is_local[side][None, :],
                jnp.take(current, local_index[side], axis=1),
                jnp.take(ghosts, ghost_index[side], axis=1),
            )
            for side in range(normals.shape[0])
        ]
        current = relax(current, neighbours, velocity, normals, params, norm_z, equilibrium)
    final = reduce_moments(current)
    return (current, final[:13])


MESH = pl.DeviceIdType.MESH
LOG2E = 1.4426950408889634
QUAD = 4
CHUNKS = 4
HI = lax.Precision.HIGHEST


def coefficient_rows(m):
    full = macroscopic_rows([m[r : r + 1, :] for r in range(13)])
    scale = -0.5 * LOG2E
    return full[:13], [row * scale for row in full[13:23]], full[23]


def macroscopic_rows(m):
    density = m[0]
    inv_d = 1.0 / density
    ux, uy, uz = (m[1] * inv_d, m[2] * inv_d, m[3] * inv_d)
    b = [m[r] * inv_d for r in range(4, 10)]
    third = [m[r] * inv_d for r in range(10, 13)]
    txx, tyy, tzz = (b[0] - ux * ux, b[1] - uy * uy, b[2] - uz * uz)
    txy, txz, tyz = (b[3] - ux * uy, b[4] - ux * uz, b[5] - uy * uz)
    temper = (txx + tyy + tzz) * (1.0 / 3.0)
    trace_b = b[0] + b[1] + b[2]
    bux = b[0] * ux + b[3] * uy + b[4] * uz
    buy = b[3] * ux + b[1] * uy + b[5] * uz
    buz = b[4] * ux + b[5] * uy + b[2] * uz
    usq = ux * ux + uy * uy + uz * uz
    qx = 0.5 * (third[0] - 2.0 * bux - ux * trace_b + 2.0 * ux * usq)
    qy = 0.5 * (third[1] - 2.0 * buy - uy * trace_b + 2.0 * uy * usq)
    qz = 0.5 * (third[2] - 2.0 * buz - uz * trace_b + 2.0 * uz * usq)
    iso = (1.0 - ellipsoid_mix) * temper
    lxx, lyy, lzz = (iso + ellipsoid_mix * txx, iso + ellipsoid_mix * tyy, iso + ellipsoid_mix * tzz)
    lxy, lxz, lyz = (ellipsoid_mix * txy, ellipsoid_mix * txz, ellipsoid_mix * tyz)
    cxx = lyy * lzz - lyz * lyz
    cxy = lyz * lxz - lxy * lzz
    cxz = lxy * lyz - lyy * lxz
    cyy = lxx * lzz - lxz * lxz
    cyz = lxy * lxz - lxx * lyz
    czz = lxx * lyy - lxy * lxy
    inv_det = 1.0 / (lxx * cxx + lxy * cxy + lxz * cxz)
    ixx, iyy, izz = (cxx * inv_det, cyy * inv_det, czz * inv_det)
    ixy, ixz, iyz = (cxy * inv_det, cxz * inv_det, cyz * inv_det)
    wx = ixx * ux + ixy * uy + ixz * uz
    wy = ixy * ux + iyy * uy + iyz * uz
    wz = ixz * ux + iyz * uy + izz * uz
    offset = ux * wx + uy * wy + uz * wz
    collide = prandtl * density * jnp.exp(visc_power * jnp.log(temper))
    return [
        density, ux, uy, uz, txx, tyy, tzz, txy, txz, tyz, qx, qy, qz,
        ixx, iyy, izz, 2.0 * ixy, 2.0 * ixz, 2.0 * iyz,
        -2.0 * wx, -2.0 * wy, -2.0 * wz, offset, collide,
    ]


def node_velocity(index, z_count):
    shift = VXY.bit_length() - 1
    centre = (VXY - 1) / 2.0
    vx = ((index & (VXY - 1)).astype(jnp.float32) - centre) * spacing
    vy = (((index >> shift) & (VXY - 1)).astype(jnp.float32) - centre) * spacing
    vz = ((index >> (2 * shift)).astype(jnp.float32) - (z_count - 1) / 2.0) * spacing
    return vx, vy, vz


def exponent_at(q, vx, vy, vz):
    return (
        vx * (q[0] * vx + q[3] * vy + q[4] * vz + q[6])
        + vy * (q[1] * vy + q[5] * vz + q[7])
        + (vz * (q[2] * vz + q[8]) + q[9])
    )


def x_column(width):
    rows = lax.broadcasted_iota(jnp.int32, (VXY, width), 0)
    return (rows.astype(jnp.float32) - (VXY - 1) / 2.0) * spacing


def gauss_total(q, width, z_count):
    vx = x_column(width)
    base = (q[0] * vx + q[6]) * vx

    def level(k, acc):
        vz = (k.astype(jnp.float32) - (z_count - 1) / 2.0) * spacing
        slope = q[4] * vz
        odd = q[5] * vz + q[7]
        even = vz * (q[2] * vz + q[8]) + q[9]
        level_base = base + vx * slope + even
        for j in range(VXY // 2):
            vy = (j + 0.5) * spacing
            mid = level_base + q[1] * (vy * vy)
            tilt = (vx * q[3] + odd) * vy
            acc = acc + (jnp.exp2(mid + tilt) + jnp.exp2(mid - tilt))
        return acc

    acc = lax.fori_loop(0, z_count, level, jnp.zeros((VXY, width), jnp.float32))
    return jnp.sum(acc, axis=0, keepdims=True)


def gauss_moments(q, width, z_count):
    vx = x_column(width)
    base = (q[0] * vx + q[6]) * vx
    zero = jnp.zeros((VXY, width), jnp.float32)

    def level(k, carry):
        vz = (k.astype(jnp.float32) - (z_count - 1) / 2.0) * spacing
        slope = q[4] * vz
        odd = q[5] * vz + q[7]
        even = vz * (q[2] * vz + q[8]) + q[9]
        level_base = base + vx * slope + even
        s0, s1, s2, s3 = (zero, zero, zero, zero)
        for j in range(VXY // 2):
            vy = (j + 0.5) * spacing
            mid = level_base + q[1] * (vy * vy)
            tilt = (vx * q[3] + odd) * vy
            up = jnp.exp2(mid + tilt)
            down = jnp.exp2(mid - tilt)
            both = up + down
            diff = (up - down) * vy
            s0 = s0 + both
            s1 = s1 + diff
            s2 = s2 + both * (vy * vy)
            s3 = s3 + diff * (vy * vy)
        z0 = vz * s0
        zz0 = vz * z0
        z1 = vz * s1
        new = (s0, s1, s2, s3, z0, zz0, z1, vz * zz0 + vz * s2, vz * z1)
        return tuple(a + b for a, b in zip(carry, new))

    s0, s1, s2, s3, z0, zz0, z1, zc, zz1 = lax.fori_loop(0, z_count, level, (zero,) * 9)
    vxx = vx * vx
    terms = [
        s0, vx * s0, s1, z0, vxx * s0, s2, zz0, vx * s1, vx * z0, z1,
        vx * (vxx * s0 + s2 + zz0), vxx * s1 + s3 + zz1, vxx * z0 + zc,
    ]
    return [jnp.sum(t, axis=0, keepdims=True) for t in terms]


def split_dot(lhs, rhs):
    return jnp.dot(lhs, rhs, precision=HI, preferred_element_type=jnp.float32)


def step_kernel(
    total_vel,
    f_ref, n_ref, adj_ref, send_ref,
    out_ref, fields_ref,
    fx, nx, adjx, sendx, oh, tr0, fnew, tr1, phi_ref,
    part0, rs0, zb0, full0, part1, rs1, zb1, full1,
    bulk_s, bulk_r, meta_s, meta_r,
    a_s, a_r, b_s, b_r, c_s, c_r,
    d_s, d_r, e_s, e_r, g_s, g_r,
):
    nodes, cells = f_ref.shape
    both = 2 * cells
    faces = n_ref.shape[0]
    z_count = total_vel // (VXY * VXY)
    rows = nodes // CHUNKS
    group = lax.axis_index("space")
    other = 1 - group
    vel = lax.axis_index("vel")
    ring = total_vel // nodes // QUAD
    me_q = lax.rem(vel, QUAD)
    me_z = vel // QUAD

    def at(space, z, q):
        return (space, z * QUAD + q)

    def q_of(step):
        return lax.rem(me_q + step, QUAD)

    def z_of(step):
        return lax.rem(me_z + step, ring)

    barrier = pltpu.get_barrier_semaphore()
    for step in range(1, QUAD):
        pl.semaphore_signal(barrier, inc=1, device_id=at(group, me_z, q_of(step)), device_id_type=MESH)
    for step in range(1, ring):
        pl.semaphore_signal(barrier, inc=1, device_id=at(group, z_of(step), me_q), device_id_type=MESH)
    for step in range(QUAD):
        pl.semaphore_signal(barrier, inc=1, device_id=at(other, me_z, q_of(step)), device_id_type=MESH)

    lane_v = node_velocity(lax.broadcasted_iota(jnp.int32, (1, nodes), 1) + vel * nodes, z_count)
    lx, ly, lz = lane_v
    sq = lx * lx + ly * ly + lz * lz
    table = [
        jnp.ones_like(lx), lx, ly, lz, lx * lx, ly * ly, lz * lz,
        lx * ly, lx * lz, ly * lz, lx * sq, ly * sq, lz * sq,
    ]
    row_id = lax.broadcasted_iota(jnp.int32, (16, nodes), 0)
    phi = jnp.zeros((16, nodes), jnp.float32)
    for r, row in enumerate(table):
        phi = jnp.where(row_id == r, row, phi)
    phi_ref[...] = phi
    inv_total = 1.0 / total_vel
    half = cells // 2
    m_part = split_dot(phi, f_ref[...]) * inv_total
    for q in range(QUAD):
        part0[q] = m_part[(q // 2) * 8 : (q // 2) * 8 + 8, (q % 2) * half : (q % 2 + 1) * half]

    pl.semaphore_wait(barrier, 2 * QUAD - 1 + ring - 1)

    def remote(src, dst, s, r, dev):
        return pltpu.make_async_remote_copy(
            src_ref=src, dst_ref=dst, send_sem=s, recv_sem=r, device_id=dev, device_id_type=MESH
        )

    pair = at(other, me_z, me_q)
    metas = [
        remote(send_ref, sendx, meta_s.at[0], meta_r.at[0], pair),
        remote(adj_ref, adjx, meta_s.at[1], meta_r.at[1], pair),
        remote(n_ref, nx, meta_s.at[2], meta_r.at[2], pair),
    ]
    for copy in metas:
        copy.start()

    def scatter(part, rs, s, r):
        copies = [
            remote(part.at[q_of(t)], rs.at[t], s.at[t], r.at[t], at(group, me_z, q_of(t)))
            for t in range(1, QUAD)
        ]
        for copy in copies:
            copy.start()
        return copies

    def along_z(zb, s, r):
        copies = [
            remote(zb.at[0], zb.at[t], s.at[t], r.at[t], at(group, z_of(t), me_q))
            for t in range(1, ring)
        ]
        for copy in copies:
            copy.start()
        return copies

    def bulk(c):
        part = pl.ds(pl.multiple_of(c * rows, rows), rows)
        return remote(f_ref.at[part], fx.at[part], bulk_s.at[c], bulk_r.at[c], pair)

    first = scatter(part0, rs0, a_s, a_r)
    for c in range(CHUNKS):
        bulk(c).start()

    for copy in metas:
        copy.wait_recv()
    slot_id = lax.broadcasted_iota(jnp.int32, (cells, cells), 0)
    cell_id = lax.broadcasted_iota(jnp.int32, (both, both), 0)

    def listed(send_row, adjacency):
        hit = (slot_id == adjacency - cells).astype(jnp.bfloat16)
        values = jnp.broadcast_to(send_row, (8, cells)).astype(jnp.float32).astype(jnp.bfloat16)
        got = jnp.dot(values, hit, preferred_element_type=jnp.float32)
        return got[0:1].astype(jnp.int32)

    to_me = sendx[0, pl.ds(group, 1), :]
    to_other = send_ref[0, pl.ds(other, 1), :]
    for k in range(faces):
        own = adj_ref[k : k + 1, :]
        theirs = adjx[k : k + 1, :]
        own = jnp.where(own < cells, own, cells + listed(to_me, own))
        theirs = jnp.where(theirs < cells, cells + theirs, listed(to_other, theirs))
        index = jnp.concatenate([own, theirs], axis=1)
        oh[k] = (cell_id == index).astype(jnp.bfloat16)

    for copy in first:
        copy.wait_recv()
    zb0[0] = part0[me_q] + rs0[1] + rs0[2] + rs0[3]
    second = along_z(zb0, b_s, b_r)
    for copy in second:
        copy.wait_recv()
    total0 = zb0[0]
    for t in range(1, ring):
        total0 = total0 + zb0[t]
    full0[0, me_q] = total0
    third = []
    for t in range(1, QUAD):
        third.append(
            remote(full0.at[0, me_q], full0.at[0, me_q], c_s.at[t], c_r.at[t], at(group, me_z, q_of(t)))
        )
    for t in range(QUAD):
        third.append(
            remote(
                full0.at[0, me_q], full0.at[1, me_q], c_s.at[QUAD + t], c_r.at[QUAD + t],
                at(other, me_z, q_of(t)),
            )
        )
    for copy in third:
        copy.start()

    def local_velocity(c, width):
        index = lax.broadcasted_iota(jnp.int32, (rows, width), 0) + (vel * nodes + c * rows)
        return node_velocity(index, z_count)

    def transport(state, c, width):
        high = state.astype(jnp.bfloat16)
        low = (state - high.astype(jnp.float32)).astype(jnp.bfloat16)
        lhs = jnp.concatenate([high, low], axis=0)
        vx, vy, vz = local_velocity(c, width)
        mine = state[:, :width]
        result = jnp.zeros((rows, width), jnp.float32)
        for k in range(faces):
            got = jnp.dot(lhs, oh[k, :, 0:width], preferred_element_type=jnp.float32)
            got = got[:rows] + got[rows:]
            normal = []
            for d in range(3):
                line = n_ref[k, d : d + 1, :]
                if width > cells:
                    line = jnp.concatenate([line, nx[k, d : d + 1, :]], axis=1)
                normal.append(line)
            speed = vx * normal[0] + vy * normal[1] + vz * normal[2]
            result = result + (jnp.maximum(speed, 0.0) * mine + jnp.minimum(speed, 0.0) * got)
        return result

    def wide(c):
        part = pl.ds(pl.multiple_of(c * rows, rows), rows)
        return part, jnp.concatenate([f_ref[part, :], fx[part, :]], axis=1)

    def first_transport(c, carry):
        bulk(c).wait_recv()
        part, state = wide(c)
        tr0[part, :] = transport(state, c, both)
        return carry

    early = CHUNKS // 2
    lax.fori_loop(0, early, first_transport, 0)
    for copy in third:
        copy.wait_recv()

    def joined(full):
        top = jnp.concatenate([full[0], full[1]], axis=1)
        bottom = jnp.concatenate([full[2], full[3]], axis=1)
        return jnp.concatenate([top, bottom], axis=0)

    mom0 = jnp.concatenate([joined(full0[0]), joined(full0[1])], axis=1)
    fields0, quad0, freq0 = coefficient_rows(mom0)
    z0 = gauss_total(quad0, both, z_count) * inv_total
    gain0 = time_step * freq0 * fields0[0] / z0
    keep0 = 1.0 - time_step * freq0

    lax.fori_loop(early, CHUNKS, first_transport, 0)

    def second_transport(c, carry):
        part, state = wide(c)
        vx, vy, vz = local_velocity(c, both)
        state = keep0 * state - time_step * tr0[part, :] + gain0 * jnp.exp2(exponent_at(quad0, vx, vy, vz))
        fnew[part, :] = state[:, :cells]
        tr1[part, :] = transport(state, c, cells)
        return carry

    lax.fori_loop(0, CHUNKS, second_transport, 0)

    phi = phi_ref[...]
    m_new = split_dot(phi, fnew[...]) * inv_total
    m_tr = split_dot(phi, tr1[...]) * inv_total
    for q in range(QUAD):
        src = m_new if q < 2 else m_tr
        part1[q] = src[:, (q % 2) * half : (q % 2 + 1) * half]
    fourth = scatter(part1, rs1, d_s, d_r)
    for copy in fourth:
        copy.wait_recv()
    zb1[0] = part1[me_q] + rs1[1] + rs1[2] + rs1[3]
    fifth = along_z(zb1, e_s, e_r)
    for copy in fifth:
        copy.wait_recv()
    total1 = zb1[0]
    for t in range(1, ring):
        total1 = total1 + zb1[t]
    full1[me_q] = total1
    sixth = [
        remote(full1.at[me_q], full1.at[me_q], g_s.at[t], g_r.at[t], at(group, me_z, q_of(t)))
        for t in range(1, QUAD)
    ]
    for copy in sixth:
        copy.start()
    for copy in sixth:
        copy.wait_recv()
    mom1 = jnp.concatenate([full1[0], full1[1]], axis=1)
    mom_t = jnp.concatenate([full1[2], full1[3]], axis=1)
    fields1, quad1, freq1 = coefficient_rows(mom1)
    sums = gauss_moments(quad1, cells, z_count)
    inv_sum = 1.0 / sums[0]
    lift = time_step * freq1 * fields1[0]
    gain1 = lift * inv_sum * float(total_vel)
    keep1 = 1.0 - time_step * freq1

    def finish(c, carry):
        part = pl.ds(pl.multiple_of(c * rows, rows), rows)
        vx, vy, vz = local_velocity(c, cells)
        out_ref[part, :] = (
            keep1 * fnew[part, :] - time_step * tr1[part, :]
            + gain1 * jnp.exp2(exponent_at(quad1, vx, vy, vz))
        )
        return carry

    lax.fori_loop(0, CHUNKS, finish, 0)
    ratio = lift * inv_sum
    last = [
        keep1 * mom1[r : r + 1] - time_step * mom_t[r : r + 1] + ratio * sums[r] for r in range(13)
    ]
    final = macroscopic_rows(last)
    for r in range(13):
        fields_ref[r : r + 1, :] = final[r]
    for c in range(CHUNKS):
        bulk(c).wait_send()
    for copy in metas + first + second + third + fourth + fifth + sixth:
        copy.wait_send()


def per_device_pair(distribution, normals, adjacency, send_list, block_counts):
    nodes, cells = distribution.shape
    size = lax.axis_size("vel")
    ring = size // QUAD
    half = cells // 2
    f32 = jnp.float32
    dma = pltpu.SemaphoreType.DMA
    vmem = pl.BlockSpec(memory_space=pltpu.VMEM)
    return pl.pallas_call(
        functools.partial(step_kernel, nodes * size),
        out_shape=(
            jax.ShapeDtypeStruct((nodes, cells), f32),
            jax.ShapeDtypeStruct((13, cells), f32),
        ),
        in_specs=[vmem] * 4,
        out_specs=(vmem, vmem),
        scratch_shapes=[
            pltpu.VMEM((nodes, cells), f32),
            pltpu.VMEM(normals.shape, f32),
            pltpu.VMEM(adjacency.shape, jnp.int32),
            pltpu.VMEM(send_list.shape, jnp.int32),
            pltpu.VMEM((normals.shape[0], 2 * cells, 2 * cells), jnp.bfloat16),
            pltpu.VMEM((nodes, 2 * cells), f32),
            pltpu.VMEM((nodes, cells), f32),
            pltpu.VMEM((nodes, cells), f32),
            pltpu.VMEM((16, nodes), f32),
            pltpu.VMEM((QUAD, 8, half), f32),
            pltpu.VMEM((QUAD, 8, half), f32),
            pltpu.VMEM((ring, 8, half), f32),
            pltpu.VMEM((2, QUAD, 8, half), f32),
            pltpu.VMEM((QUAD, 16, half), f32),
            pltpu.VMEM((QUAD, 16, half), f32),
            pltpu.VMEM((ring, 16, half), f32),
            pltpu.VMEM((QUAD, 16, half), f32),
            dma((CHUNKS,)), dma((CHUNKS,)), dma((3,)), dma((3,)),
            dma((QUAD,)), dma((QUAD,)), dma((ring,)), dma((ring,)), dma((2 * QUAD,)), dma((2 * QUAD,)),
            dma((QUAD,)), dma((QUAD,)), dma((ring,)), dma((ring,)), dma((QUAD,)), dma((QUAD,)),
        ],
        compiler_params=pltpu.CompilerParams(collective_id=0, has_side_effects=True),
        name="steps",
    )(distribution, normals, adjacency, send_list)


def solution(mesh):
    placed = (
        P("vel", "space"),
        P(None, None, "space"),
        P(None, "space"),
        P("space", None, None),
        P(None, "space"),
    )
    pair = mesh.shape["space"] == 2 and mesh.shape["vel"] % QUAD == 0 and ITERS == 2
    return jax.shard_map(
        per_device_pair if pair else per_device,
        mesh=mesh,
        in_specs=placed,
        out_specs=(P("vel", "space"), P(None, "space")),
        check_vma=False,
    )
```

```python
import functools

import jax
import jax.numpy as jnp
from jax import lax
from jax.experimental import pallas as pl
from jax.experimental.pallas import tpu as pltpu
from jax.sharding import PartitionSpec as P

VXY = 32
TILE = 128
ITERS = 2


spacing = 0.3
ellipsoid_mix = -0.25
prandtl = 0.8
visc_power = 0.26
time_step = 0.025


def velocity_nodes(vel_index, z_count):
    comp_x = (vel_index % VXY).astype(jnp.float32)
    comp_y = (vel_index // VXY % VXY).astype(jnp.float32)
    comp_z = (vel_index // (VXY * VXY)).astype(jnp.float32)
    centre = (VXY - 1) / 2.0
    return jnp.stack(
        [
            (comp_x - centre) * spacing,
            (comp_y - centre) * spacing,
            (comp_z - (z_count - 1) / 2.0) * spacing,
        ]
    )


def moment_rows(velocity):
    comp_x, comp_y, comp_z = (velocity[0], velocity[1], velocity[2])
    squared = comp_x * comp_x + comp_y * comp_y + comp_z * comp_z
    return jnp.stack(
        [
            jnp.ones_like(comp_x),
            comp_x,
            comp_y,
            comp_z,
            comp_x * comp_x,
            comp_y * comp_y,
            comp_z * comp_z,
            comp_x * comp_y,
            comp_x * comp_z,
            comp_y * comp_z,
            comp_x * squared,
            comp_y * squared,
            comp_z * squared,
        ]
    )


def quad_rows(velocity):
    comp_x, comp_y, comp_z = (velocity[0], velocity[1], velocity[2])
    return jnp.stack(
        [
            comp_x * comp_x,
            comp_y * comp_y,
            comp_z * comp_z,
            comp_x * comp_y,
            comp_x * comp_z,
            comp_y * comp_z,
            comp_x,
            comp_y,
            comp_z,
            jnp.ones_like(comp_x),
        ]
    )


def macroscopic(moments):
    density = moments[0]
    mean_x = moments[1] / density
    mean_y = moments[2] / density
    mean_z = moments[3] / density
    second = moments[4:10] / density[None, :]
    third = moments[10:13] / density[None, :]
    theta_xx = second[0] - mean_x * mean_x
    theta_yy = second[1] - mean_y * mean_y
    theta_zz = second[2] - mean_z * mean_z
    theta_xy = second[3] - mean_x * mean_y
    theta_xz = second[4] - mean_x * mean_z
    theta_yz = second[5] - mean_y * mean_z
    temper = (theta_xx + theta_yy + theta_zz) / 3.0
    trace_b = second[0] + second[1] + second[2]
    bu_x = second[0] * mean_x + second[3] * mean_y + second[4] * mean_z
    bu_y = second[3] * mean_x + second[1] * mean_y + second[5] * mean_z
    bu_z = second[4] * mean_x + second[5] * mean_y + second[2] * mean_z
    mean_sq = mean_x * mean_x + mean_y * mean_y + mean_z * mean_z
    flux_x = 0.5 * (third[0] - 2.0 * bu_x - mean_x * trace_b + 2.0 * mean_x * mean_sq)
    flux_y = 0.5 * (third[1] - 2.0 * bu_y - mean_y * trace_b + 2.0 * mean_y * mean_sq)
    flux_z = 0.5 * (third[2] - 2.0 * bu_z - mean_z * trace_b + 2.0 * mean_z * mean_sq)
    iso_part = (1.0 - ellipsoid_mix) * temper
    lam_xx = iso_part + ellipsoid_mix * theta_xx
    lam_yy = iso_part + ellipsoid_mix * theta_yy
    lam_zz = iso_part + ellipsoid_mix * theta_zz
    lam_xy = ellipsoid_mix * theta_xy
    lam_xz = ellipsoid_mix * theta_xz
    lam_yz = ellipsoid_mix * theta_yz
    cof_xx = lam_yy * lam_zz - lam_yz * lam_yz
    cof_xy = lam_yz * lam_xz - lam_xy * lam_zz
    cof_xz = lam_xy * lam_yz - lam_yy * lam_xz
    cof_yy = lam_xx * lam_zz - lam_xz * lam_xz
    cof_yz = lam_xy * lam_xz - lam_xx * lam_yz
    cof_zz = lam_xx * lam_yy - lam_xy * lam_xy
    determinant = lam_xx * cof_xx + lam_xy * cof_xy + lam_xz * cof_xz
    inv_xx = cof_xx / determinant
    inv_yy = cof_yy / determinant
    inv_zz = cof_zz / determinant
    inv_xy = cof_xy / determinant
    inv_xz = cof_xz / determinant
    inv_yz = cof_yz / determinant
    lin_x = inv_xx * mean_x + inv_xy * mean_y + inv_xz * mean_z
    lin_y = inv_xy * mean_x + inv_yy * mean_y + inv_yz * mean_z
    lin_z = inv_xz * mean_x + inv_yz * mean_y + inv_zz * mean_z
    offset = mean_x * lin_x + mean_y * lin_y + mean_z * lin_z
    collide = prandtl * density * jnp.exp(visc_power * jnp.log(temper))
    return jnp.stack(
        [
            density,
            mean_x,
            mean_y,
            mean_z,
            theta_xx,
            theta_yy,
            theta_zz,
            theta_xy,
            theta_xz,
            theta_yz,
            flux_x,
            flux_y,
            flux_z,
            inv_xx,
            inv_yy,
            inv_zz,
            2.0 * inv_xy,
            2.0 * inv_xz,
            2.0 * inv_yz,
            -2.0 * lin_x,
            -2.0 * lin_y,
            -2.0 * lin_z,
            offset,
            collide,
        ]
    )


def ghost_slots(adjacency, counts, cells, groups, slot_count):
    ends = jnp.cumsum(counts) * TILE
    starts = ends - counts * TILE
    is_local = adjacency < cells
    position = jnp.maximum(adjacency - cells, 0)
    source = jnp.sum((ends[:, None, None] <= position[None]).astype(jnp.int32), axis=0)
    source = jnp.minimum(source, groups - 1)
    group_ids = jnp.arange(groups, dtype=jnp.int32)[:, None, None]
    chosen = jnp.sum(jnp.where(group_ids == source[None], starts[:, None, None], 0), axis=0)
    slot_pos = jnp.clip(position - chosen, 0, slot_count - 1)
    return (is_local, source, slot_pos)


def relax(current, neighbours, velocity, normals, params, norm_z, equilibrium):
    gauss = params[0][None, :] * equilibrium / norm_z[None, :]
    outflow = jnp.zeros(current.shape, jnp.float32)
    inflow = jnp.zeros(current.shape, jnp.float32)
    for side in range(normals.shape[0]):
        normal_speed = (
            velocity[0][:, None] * normals[side, 0][None, :]
            + velocity[1][:, None] * normals[side, 1][None, :]
            + velocity[2][:, None] * normals[side, 2][None, :]
        )
        outflow = outflow + jnp.maximum(normal_speed, 0.0)
        inflow = inflow + jnp.minimum(normal_speed, 0.0) * neighbours[side]
    return current + time_step * (
        params[23][None, :] * (gauss - current) - outflow * current - inflow
    )


def per_device(distribution, normals, adjacency, send_list, block_counts):
    vel_local = distribution.shape[0]
    cells = distribution.shape[1]
    total_vel = vel_local * lax.axis_size("vel")
    z_count = total_vel // (VXY * VXY)
    groups = send_list.shape[1]
    slot_count = send_list.shape[2]
    vel_index = lax.axis_index("vel") * vel_local + jnp.arange(vel_local, dtype=jnp.int32)
    velocity = velocity_nodes(vel_index, z_count)
    moment_table = moment_rows(velocity)
    quad_table = quad_rows(velocity).T
    is_local, source, slot_pos = ghost_slots(
        adjacency, block_counts[:, 0], cells, groups, slot_count
    )
    ghost_index = source * slot_count + slot_pos
    local_index = jnp.where(is_local, adjacency, 0)
    send_rows = send_list[0].reshape(-1)

    def reduce_moments(current):
        partial_value = (
            jnp.dot(
                moment_table,
                current,
                precision=lax.Precision.HIGHEST,
                preferred_element_type=jnp.float32,
            )
            / total_vel
        )
        return macroscopic(lax.psum(partial_value, "vel"))

    current = distribution
    for iteration in range(ITERS):
        params = reduce_moments(current)
        ghosts = lax.all_to_all(
            jnp.take(current, send_rows, axis=1), "space", split_axis=1, concat_axis=1, tiled=True
        )
        exponent = jnp.dot(
            quad_table,
            params[13:23],
            precision=lax.Precision.HIGHEST,
            preferred_element_type=jnp.float32,
        )
        equilibrium = jnp.exp(-0.5 * exponent)
        norm_z = lax.psum(jnp.sum(equilibrium, axis=0) / total_vel, "vel")
        neighbours = [
            jnp.where(
                is_local[side][None, :],
                jnp.take(current, local_index[side], axis=1),
                jnp.take(ghosts, ghost_index[side], axis=1),
            )
            for side in range(normals.shape[0])
        ]
        current = relax(current, neighbours, velocity, normals, params, norm_z, equilibrium)
    final = reduce_moments(current)
    return (current, final[:13])


MESH = pl.DeviceIdType.MESH
LOG2E = 1.4426950408889634
QUAD = 4
CHUNKS = 4
HI = lax.Precision.HIGHEST


def coefficient_rows(m):
    full = macroscopic_rows([m[r : r + 1, :] for r in range(13)])
    scale = -0.5 * LOG2E
    return full[:13], [row * scale for row in full[13:23]], full[23]


def macroscopic_rows(m):
    density = m[0]
    inv_d = 1.0 / density
    ux, uy, uz = (m[1] * inv_d, m[2] * inv_d, m[3] * inv_d)
    b = [m[r] * inv_d for r in range(4, 10)]
    third = [m[r] * inv_d for r in range(10, 13)]
    txx, tyy, tzz = (b[0] - ux * ux, b[1] - uy * uy, b[2] - uz * uz)
    txy, txz, tyz = (b[3] - ux * uy, b[4] - ux * uz, b[5] - uy * uz)
    temper = (txx + tyy + tzz) * (1.0 / 3.0)
    trace_b = b[0] + b[1] + b[2]
    bux = b[0] * ux + b[3] * uy + b[4] * uz
    buy = b[3] * ux + b[1] * uy + b[5] * uz
    buz = b[4] * ux + b[5] * uy + b[2] * uz
    usq = ux * ux + uy * uy + uz * uz
    qx = 0.5 * (third[0] - 2.0 * bux - ux * trace_b + 2.0 * ux * usq)
    qy = 0.5 * (third[1] - 2.0 * buy - uy * trace_b + 2.0 * uy * usq)
    qz = 0.5 * (third[2] - 2.0 * buz - uz * trace_b + 2.0 * uz * usq)
    iso = (1.0 - ellipsoid_mix) * temper
    lxx, lyy, lzz = (iso + ellipsoid_mix * txx, iso + ellipsoid_mix * tyy, iso + ellipsoid_mix * tzz)
    lxy, lxz, lyz = (ellipsoid_mix * txy, ellipsoid_mix * txz, ellipsoid_mix * tyz)
    cxx = lyy * lzz - lyz * lyz
    cxy = lyz * lxz - lxy * lzz
    cxz = lxy * lyz - lyy * lxz
    cyy = lxx * lzz - lxz * lxz
    cyz = lxy * lxz - lxx * lyz
    czz = lxx * lyy - lxy * lxy
    inv_det = 1.0 / (lxx * cxx + lxy * cxy + lxz * cxz)
    ixx, iyy, izz = (cxx * inv_det, cyy * inv_det, czz * inv_det)
    ixy, ixz, iyz = (cxy * inv_det, cxz * inv_det, cyz * inv_det)
    wx = ixx * ux + ixy * uy + ixz * uz
    wy = ixy * ux + iyy * uy + iyz * uz
    wz = ixz * ux + iyz * uy + izz * uz
    offset = ux * wx + uy * wy + uz * wz
    collide = prandtl * density * jnp.exp(visc_power * jnp.log(temper))
    return [
        density, ux, uy, uz, txx, tyy, tzz, txy, txz, tyz, qx, qy, qz,
        ixx, iyy, izz, 2.0 * ixy, 2.0 * ixz, 2.0 * iyz,
        -2.0 * wx, -2.0 * wy, -2.0 * wz, offset, collide,
    ]


def node_velocity(index, z_count):
    shift = VXY.bit_length() - 1
    centre = (VXY - 1) / 2.0
    vx = ((index & (VXY - 1)).astype(jnp.float32) - centre) * spacing
    vy = (((index >> shift) & (VXY - 1)).astype(jnp.float32) - centre) * spacing
    vz = ((index >> (2 * shift)).astype(jnp.float32) - (z_count - 1) / 2.0) * spacing
    return vx, vy, vz


def exponent_at(q, vx, vy, vz):
    return (
        vx * (q[0] * vx + q[3] * vy + q[4] * vz + q[6])
        + vy * (q[1] * vy + q[5] * vz + q[7])
        + (vz * (q[2] * vz + q[8]) + q[9])
    )


def x_column(width):
    rows = lax.broadcasted_iota(jnp.int32, (VXY, width), 0)
    return (rows.astype(jnp.float32) - (VXY - 1) / 2.0) * spacing


def gauss_total(q, width, z_count):
    vx = x_column(width)
    base = (q[0] * vx + q[6]) * vx

    def level(k, acc):
        vz = (k.astype(jnp.float32) - (z_count - 1) / 2.0) * spacing
        slope = q[4] * vz
        odd = q[5] * vz + q[7]
        even = vz * (q[2] * vz + q[8]) + q[9]
        level_base = base + vx * slope + even
        for j in range(VXY // 2):
            vy = (j + 0.5) * spacing
            mid = level_base + q[1] * (vy * vy)
            tilt = (vx * q[3] + odd) * vy
            acc = acc + (jnp.exp2(mid + tilt) + jnp.exp2(mid - tilt))
        return acc

    acc = lax.fori_loop(0, z_count, level, jnp.zeros((VXY, width), jnp.float32))
    return jnp.sum(acc, axis=0, keepdims=True)


def gauss_moments(q, width, z_count):
    vx = x_column(width)
    base = (q[0] * vx + q[6]) * vx
    zero = jnp.zeros((VXY, width), jnp.float32)

    def level(k, carry):
        vz = (k.astype(jnp.float32) - (z_count - 1) / 2.0) * spacing
        slope = q[4] * vz
        odd = q[5] * vz + q[7]
        even = vz * (q[2] * vz + q[8]) + q[9]
        level_base = base + vx * slope + even
        s0, s1, s2, s3 = (zero, zero, zero, zero)
        for j in range(VXY // 2):
            vy = (j + 0.5) * spacing
            mid = level_base + q[1] * (vy * vy)
            tilt = (vx * q[3] + odd) * vy
            up = jnp.exp2(mid + tilt)
            down = jnp.exp2(mid - tilt)
            both = up + down
            diff = (up - down) * vy
            s0 = s0 + both
            s1 = s1 + diff
            s2 = s2 + both * (vy * vy)
            s3 = s3 + diff * (vy * vy)
        z0 = vz * s0
        zz0 = vz * z0
        z1 = vz * s1
        new = (s0, s1, s2, s3, z0, zz0, z1, vz * zz0 + vz * s2, vz * z1)
        return tuple(a + b for a, b in zip(carry, new))

    s0, s1, s2, s3, z0, zz0, z1, zc, zz1 = lax.fori_loop(0, z_count, level, (zero,) * 9)
    vxx = vx * vx
    terms = [
        s0, vx * s0, s1, z0, vxx * s0, s2, zz0, vx * s1, vx * z0, z1,
        vx * (vxx * s0 + s2 + zz0), vxx * s1 + s3 + zz1, vxx * z0 + zc,
    ]
    return [jnp.sum(t, axis=0, keepdims=True) for t in terms]


def split_dot(lhs, rhs):
    return jnp.dot(lhs, rhs, precision=HI, preferred_element_type=jnp.float32)


def step_kernel(
    total_vel,
    f_ref, n_ref, adj_ref, send_ref,
    out_ref, fields_ref,
    fx, nx, adjx, sendx, oh, tr0, fnew, tr1, phi_ref,
    qb0, zb0, total_mine, total_theirs, qb1, zb1, qb2, zb2,
    bulk_s, bulk_r, meta_s, meta_r,
    a_s, a_r, b_s, b_r, x_s, x_r,
    d_s, d_r, e_s, e_r, g_s, g_r, h_s, h_r,
):
    nodes, cells = f_ref.shape
    both = 2 * cells
    faces = n_ref.shape[1]
    z_count = total_vel // (VXY * VXY)
    rows = nodes // CHUNKS
    group = lax.axis_index("space")
    other = 1 - group
    vel = lax.axis_index("vel")
    ring = total_vel // nodes // QUAD
    me_q = lax.rem(vel, QUAD)
    me_z = vel // QUAD

    def at(space, z, q):
        return (space, z * QUAD + q)

    def q_of(step):
        return lax.rem(me_q + step, QUAD)

    def z_of(step):
        return lax.rem(me_z + step, ring)

    barrier = pltpu.get_barrier_semaphore()
    for step in range(1, QUAD):
        pl.semaphore_signal(barrier, inc=1, device_id=at(group, me_z, q_of(step)), device_id_type=MESH)
    for step in range(1, ring):
        pl.semaphore_signal(barrier, inc=1, device_id=at(group, z_of(step), me_q), device_id_type=MESH)
    pl.semaphore_signal(barrier, inc=1, device_id=at(other, me_z, me_q), device_id_type=MESH)

    lane_v = node_velocity(lax.broadcasted_iota(jnp.int32, (1, nodes), 1) + vel * nodes, z_count)
    lx, ly, lz = lane_v
    sq = lx * lx + ly * ly + lz * lz
    table = [
        jnp.ones_like(lx), lx, ly, lz, lx * lx, ly * ly, lz * lz,
        lx * ly, lx * lz, ly * lz, lx * sq, ly * sq, lz * sq,
    ]
    row_id = lax.broadcasted_iota(jnp.int32, (16, nodes), 0)
    phi = jnp.zeros((16, nodes), jnp.float32)
    for r, row in enumerate(table):
        phi = jnp.where(row_id == r, row, phi)
    phi_ref[...] = phi
    inv_total = 1.0 / total_vel
    qb0[me_q] = split_dot(phi, f_ref[...]) * inv_total

    pl.semaphore_wait(barrier, QUAD + ring - 1)

    def remote(src, dst, s, r, dev):
        return pltpu.make_async_remote_copy(
            src_ref=src, dst_ref=dst, send_sem=s, recv_sem=r, device_id=dev, device_id_type=MESH
        )

    pair = at(other, me_z, me_q)
    metas = [
        remote(send_ref, sendx, meta_s.at[0], meta_r.at[0], pair),
        remote(adj_ref, adjx, meta_s.at[1], meta_r.at[1], pair),
        remote(n_ref, nx, meta_s.at[2], meta_r.at[2], pair),
    ]
    for copy in metas:
        copy.start()

    def in_quad(buffer, s, r):
        copies = [
            remote(buffer.at[me_q], buffer.at[me_q], s.at[t], r.at[t], at(group, me_z, q_of(t)))
            for t in range(1, QUAD)
        ]
        for copy in copies:
            copy.start()
        return copies

    def along_z(buffer, s, r):
        copies = [
            remote(buffer.at[me_z], buffer.at[me_z], s.at[t], r.at[t], at(group, z_of(t), me_q))
            for t in range(1, ring)
        ]
        for copy in copies:
            copy.start()
        return copies

    def collect(copies, buffer, count):
        for copy in copies:
            copy.wait_recv()
        result = buffer[0]
        for t in range(1, count):
            result = result + buffer[t]
        return result

    def bulk(c):
        part = pl.ds(pl.multiple_of(c * rows, rows), rows)
        return remote(f_ref.at[part], fx.at[part], bulk_s.at[c], bulk_r.at[c], pair)

    first = in_quad(qb0, a_s, a_r)
    for c in range(CHUNKS - 1):
        bulk(c).start()

    for copy in metas:
        copy.wait_recv()
    slot_id = lax.broadcasted_iota(jnp.int32, (cells, cells), 0)
    cell_id = lax.broadcasted_iota(jnp.int32, (both, both), 0)

    def listed(send_row, adjacency):
        hit = (slot_id == adjacency - cells).astype(jnp.bfloat16)
        values = jnp.broadcast_to(send_row, (8, cells)).astype(jnp.float32).astype(jnp.bfloat16)
        got = jnp.dot(values, hit, preferred_element_type=jnp.float32)
        return got[0:1].astype(jnp.int32)

    to_me = sendx[0, pl.ds(group, 1), :]
    to_other = send_ref[0, pl.ds(other, 1), :]
    for k in range(faces):
        own = adj_ref[k : k + 1, :]
        theirs = adjx[k : k + 1, :]
        own = jnp.where(own < cells, own, cells + listed(to_me, own))
        theirs = jnp.where(theirs < cells, cells + theirs, listed(to_other, theirs))
        index = jnp.concatenate([own, theirs], axis=1)
        oh[k] = (cell_id == index).astype(jnp.bfloat16)

    zb0[me_z] = collect(first, qb0, QUAD)
    second = along_z(zb0, b_s, b_r)

    def local_velocity(c, width):
        index = lax.broadcasted_iota(jnp.int32, (rows, width), 0) + (vel * nodes + c * rows)
        return node_velocity(index, z_count)

    def transport(state, c, width):
        high = state.astype(jnp.bfloat16)
        low = (state - high.astype(jnp.float32)).astype(jnp.bfloat16)
        lhs = jnp.concatenate([high, low], axis=0)
        vx, vy, vz = local_velocity(c, width)
        mine = state[:, :width]
        result = jnp.zeros((rows, width), jnp.float32)
        for k in range(faces):
            got = jnp.dot(lhs, oh[k, :, 0:width], preferred_element_type=jnp.float32)
            got = got[:rows] + got[rows:]
            normal = []
            for d in range(3):
                line = n_ref[d, k : k + 1, :]
                if width > cells:
                    line = jnp.concatenate([line, nx[d, k : k + 1, :]], axis=1)
                normal.append(line)
            speed = vx * normal[0] + vy * normal[1] + vz * normal[2]
            result = result + (jnp.maximum(speed, 0.0) * mine + jnp.minimum(speed, 0.0) * got)
        return result

    def wide(c):
        part = pl.ds(pl.multiple_of(c * rows, rows), rows)
        return part, jnp.concatenate([f_ref[part, :], fx[part, :]], axis=1)

    def first_transport(c, carry):
        bulk(c).wait_recv()
        part, state = wide(c)
        tr0[part, :] = transport(state, c, both)
        return carry

    lax.fori_loop(0, 1, first_transport, 0)
    total_mine[...] = collect(second, zb0, ring)
    third = [remote(total_mine, total_theirs, x_s, x_r, pair)]
    third[0].start()
    bulk(CHUNKS - 1).start()

    def step_rows(moments):
        fields, quad, freq = coefficient_rows(moments)
        norm = gauss_total(quad, cells, z_count) * inv_total
        return quad, time_step * freq * fields[0] / norm, 1.0 - time_step * freq

    own_quad, own_gain, own_keep = step_rows(total_mine[...])
    lax.fori_loop(1, CHUNKS - 1, first_transport, 0)
    third[0].wait_recv()
    their_quad, their_gain, their_keep = step_rows(total_theirs[...])
    quad0 = [jnp.concatenate([a, b], axis=1) for a, b in zip(own_quad, their_quad)]
    gain0 = jnp.concatenate([own_gain, their_gain], axis=1)
    keep0 = jnp.concatenate([own_keep, their_keep], axis=1)
    lax.fori_loop(CHUNKS - 1, CHUNKS, first_transport, 0)

    def second_transport(c, carry):
        part, state = wide(c)
        vx, vy, vz = local_velocity(c, both)
        state = keep0 * state - time_step * tr0[part, :] + gain0 * jnp.exp2(exponent_at(quad0, vx, vy, vz))
        fnew[part, :] = state[:, :cells]
        tr1[part, :] = transport(state, c, cells)
        return carry

    lax.fori_loop(0, CHUNKS, second_transport, 0)

    phi = phi_ref[...]
    qb1[me_q] = split_dot(phi, fnew[...]) * inv_total
    fourth = in_quad(qb1, d_s, d_r)
    qb2[me_q] = split_dot(phi, tr1[...]) * inv_total
    fifth = in_quad(qb2, e_s, e_r)
    zb1[me_z] = collect(fourth, qb1, QUAD)
    sixth = along_z(zb1, g_s, g_r)
    zb2[me_z] = collect(fifth, qb2, QUAD)
    seventh = along_z(zb2, h_s, h_r)
    mom1 = collect(sixth, zb1, ring)
    fields1, quad1, freq1 = coefficient_rows(mom1)
    sums = gauss_moments(quad1, cells, z_count)
    inv_sum = 1.0 / sums[0]
    lift = time_step * freq1 * fields1[0]
    gain1 = lift * inv_sum * float(total_vel)
    keep1 = 1.0 - time_step * freq1

    def finish(c, carry):
        part = pl.ds(pl.multiple_of(c * rows, rows), rows)
        vx, vy, vz = local_velocity(c, cells)
        out_ref[part, :] = (
            keep1 * fnew[part, :] - time_step * tr1[part, :]
            + gain1 * jnp.exp2(exponent_at(quad1, vx, vy, vz))
        )
        return carry

    lax.fori_loop(0, CHUNKS, finish, 0)
    mom_t = collect(seventh, zb2, ring)
    ratio = lift * inv_sum
    last = [
        keep1 * mom1[r : r + 1] - time_step * mom_t[r : r + 1] + ratio * sums[r] for r in range(13)
    ]
    final = macroscopic_rows(last)
    for r in range(13):
        fields_ref[r : r + 1, :] = final[r]
    for c in range(CHUNKS):
        bulk(c).wait_send()
    for copy in metas + first + second + third + fourth + fifth + sixth + seventh:
        copy.wait_send()


def per_device_pair(distribution, normals, adjacency, send_list, block_counts):
    nodes, cells = distribution.shape
    normals = normals.transpose(1, 0, 2)
    size = lax.axis_size("vel")
    ring = size // QUAD
    f32 = jnp.float32
    dma = pltpu.SemaphoreType.DMA
    vmem = pl.BlockSpec(memory_space=pltpu.VMEM)
    return pl.pallas_call(
        functools.partial(step_kernel, nodes * size),
        out_shape=(
            jax.ShapeDtypeStruct((nodes, cells), f32),
            jax.ShapeDtypeStruct((13, cells), f32),
        ),
        in_specs=[vmem] * 4,
        out_specs=(vmem, vmem),
        scratch_shapes=[
            pltpu.VMEM((nodes, cells), f32),
            pltpu.VMEM(normals.shape, f32),
            pltpu.VMEM(adjacency.shape, jnp.int32),
            pltpu.VMEM(send_list.shape, jnp.int32),
            pltpu.VMEM((normals.shape[1], 2 * cells, 2 * cells), jnp.bfloat16),
            pltpu.VMEM((nodes, 2 * cells), f32),
            pltpu.VMEM((nodes, cells), f32),
            pltpu.VMEM((nodes, cells), f32),
            pltpu.VMEM((16, nodes), f32),
            pltpu.VMEM((QUAD, 16, cells), f32),
            pltpu.VMEM((ring, 16, cells), f32),
            pltpu.VMEM((16, cells), f32),
            pltpu.VMEM((16, cells), f32),
            pltpu.VMEM((QUAD, 16, cells), f32),
            pltpu.VMEM((ring, 16, cells), f32),
            pltpu.VMEM((QUAD, 16, cells), f32),
            pltpu.VMEM((ring, 16, cells), f32),
            dma((CHUNKS,)), dma((CHUNKS,)), dma((3,)), dma((3,)),
            dma((QUAD,)), dma((QUAD,)), dma((ring,)), dma((ring,)), dma, dma,
            dma((QUAD,)), dma((QUAD,)), dma((QUAD,)), dma((QUAD,)),
            dma((ring,)), dma((ring,)), dma((ring,)), dma((ring,)),
        ],
        compiler_params=pltpu.CompilerParams(collective_id=0, has_side_effects=True),
        name="steps",
    )(distribution, normals, adjacency, send_list)


def solution(mesh):
    placed = (
        P("vel", "space"),
        P(None, None, "space"),
        P(None, "space"),
        P("space", None, None),
        P(None, "space"),
    )
    pair = mesh.shape["space"] == 2 and mesh.shape["vel"] % QUAD == 0 and ITERS == 2
    return jax.shard_map(
        per_device_pair if pair else per_device,
        mesh=mesh,
        in_specs=placed,
        out_specs=(P("vel", "space"), P(None, "space")),
        check_vma=False,
    )
```

```python
import functools

import jax
import jax.numpy as jnp
from jax import lax
from jax.experimental import pallas as pl
from jax.experimental.pallas import tpu as pltpu
from jax.sharding import PartitionSpec as P

VXY = 32
TILE = 128
ITERS = 2


spacing = 0.3
ellipsoid_mix = -0.25
prandtl = 0.8
visc_power = 0.26
time_step = 0.025


def velocity_nodes(vel_index, z_count):
    comp_x = (vel_index % VXY).astype(jnp.float32)
    comp_y = (vel_index // VXY % VXY).astype(jnp.float32)
    comp_z = (vel_index // (VXY * VXY)).astype(jnp.float32)
    centre = (VXY - 1) / 2.0
    return jnp.stack(
        [
            (comp_x - centre) * spacing,
            (comp_y - centre) * spacing,
            (comp_z - (z_count - 1) / 2.0) * spacing,
        ]
    )


def moment_rows(velocity):
    comp_x, comp_y, comp_z = (velocity[0], velocity[1], velocity[2])
    squared = comp_x * comp_x + comp_y * comp_y + comp_z * comp_z
    return jnp.stack(
        [
            jnp.ones_like(comp_x),
            comp_x,
            comp_y,
            comp_z,
            comp_x * comp_x,
            comp_y * comp_y,
            comp_z * comp_z,
            comp_x * comp_y,
            comp_x * comp_z,
            comp_y * comp_z,
            comp_x * squared,
            comp_y * squared,
            comp_z * squared,
        ]
    )


def quad_rows(velocity):
    comp_x, comp_y, comp_z = (velocity[0], velocity[1], velocity[2])
    return jnp.stack(
        [
            comp_x * comp_x,
            comp_y * comp_y,
            comp_z * comp_z,
            comp_x * comp_y,
            comp_x * comp_z,
            comp_y * comp_z,
            comp_x,
            comp_y,
            comp_z,
            jnp.ones_like(comp_x),
        ]
    )


def macroscopic(moments):
    density = moments[0]
    mean_x = moments[1] / density
    mean_y = moments[2] / density
    mean_z = moments[3] / density
    second = moments[4:10] / density[None, :]
    third = moments[10:13] / density[None, :]
    theta_xx = second[0] - mean_x * mean_x
    theta_yy = second[1] - mean_y * mean_y
    theta_zz = second[2] - mean_z * mean_z
    theta_xy = second[3] - mean_x * mean_y
    theta_xz = second[4] - mean_x * mean_z
    theta_yz = second[5] - mean_y * mean_z
    temper = (theta_xx + theta_yy + theta_zz) / 3.0
    trace_b = second[0] + second[1] + second[2]
    bu_x = second[0] * mean_x + second[3] * mean_y + second[4] * mean_z
    bu_y = second[3] * mean_x + second[1] * mean_y + second[5] * mean_z
    bu_z = second[4] * mean_x + second[5] * mean_y + second[2] * mean_z
    mean_sq = mean_x * mean_x + mean_y * mean_y + mean_z * mean_z
    flux_x = 0.5 * (third[0] - 2.0 * bu_x - mean_x * trace_b + 2.0 * mean_x * mean_sq)
    flux_y = 0.5 * (third[1] - 2.0 * bu_y - mean_y * trace_b + 2.0 * mean_y * mean_sq)
    flux_z = 0.5 * (third[2] - 2.0 * bu_z - mean_z * trace_b + 2.0 * mean_z * mean_sq)
    iso_part = (1.0 - ellipsoid_mix) * temper
    lam_xx = iso_part + ellipsoid_mix * theta_xx
    lam_yy = iso_part + ellipsoid_mix * theta_yy
    lam_zz = iso_part + ellipsoid_mix * theta_zz
    lam_xy = ellipsoid_mix * theta_xy
    lam_xz = ellipsoid_mix * theta_xz
    lam_yz = ellipsoid_mix * theta_yz
    cof_xx = lam_yy * lam_zz - lam_yz * lam_yz
    cof_xy = lam_yz * lam_xz - lam_xy * lam_zz
    cof_xz = lam_xy * lam_yz - lam_yy * lam_xz
    cof_yy = lam_xx * lam_zz - lam_xz * lam_xz
    cof_yz = lam_xy * lam_xz - lam_xx * lam_yz
    cof_zz = lam_xx * lam_yy - lam_xy * lam_xy
    determinant = lam_xx * cof_xx + lam_xy * cof_xy + lam_xz * cof_xz
    inv_xx = cof_xx / determinant
    inv_yy = cof_yy / determinant
    inv_zz = cof_zz / determinant
    inv_xy = cof_xy / determinant
    inv_xz = cof_xz / determinant
    inv_yz = cof_yz / determinant
    lin_x = inv_xx * mean_x + inv_xy * mean_y + inv_xz * mean_z
    lin_y = inv_xy * mean_x + inv_yy * mean_y + inv_yz * mean_z
    lin_z = inv_xz * mean_x + inv_yz * mean_y + inv_zz * mean_z
    offset = mean_x * lin_x + mean_y * lin_y + mean_z * lin_z
    collide = prandtl * density * jnp.exp(visc_power * jnp.log(temper))
    return jnp.stack(
        [
            density,
            mean_x,
            mean_y,
            mean_z,
            theta_xx,
            theta_yy,
            theta_zz,
            theta_xy,
            theta_xz,
            theta_yz,
            flux_x,
            flux_y,
            flux_z,
            inv_xx,
            inv_yy,
            inv_zz,
            2.0 * inv_xy,
            2.0 * inv_xz,
            2.0 * inv_yz,
            -2.0 * lin_x,
            -2.0 * lin_y,
            -2.0 * lin_z,
            offset,
            collide,
        ]
    )


def ghost_slots(adjacency, counts, cells, groups, slot_count):
    ends = jnp.cumsum(counts) * TILE
    starts = ends - counts * TILE
    is_local = adjacency < cells
    position = jnp.maximum(adjacency - cells, 0)
    source = jnp.sum((ends[:, None, None] <= position[None]).astype(jnp.int32), axis=0)
    source = jnp.minimum(source, groups - 1)
    group_ids = jnp.arange(groups, dtype=jnp.int32)[:, None, None]
    chosen = jnp.sum(jnp.where(group_ids == source[None], starts[:, None, None], 0), axis=0)
    slot_pos = jnp.clip(position - chosen, 0, slot_count - 1)
    return (is_local, source, slot_pos)


def relax(current, neighbours, velocity, normals, params, norm_z, equilibrium):
    gauss = params[0][None, :] * equilibrium / norm_z[None, :]
    outflow = jnp.zeros(current.shape, jnp.float32)
    inflow = jnp.zeros(current.shape, jnp.float32)
    for side in range(normals.shape[0]):
        normal_speed = (
            velocity[0][:, None] * normals[side, 0][None, :]
            + velocity[1][:, None] * normals[side, 1][None, :]
            + velocity[2][:, None] * normals[side, 2][None, :]
        )
        outflow = outflow + jnp.maximum(normal_speed, 0.0)
        inflow = inflow + jnp.minimum(normal_speed, 0.0) * neighbours[side]
    return current + time_step * (
        params[23][None, :] * (gauss - current) - outflow * current - inflow
    )


def per_device(distribution, normals, adjacency, send_list, block_counts):
    vel_local = distribution.shape[0]
    cells = distribution.shape[1]
    total_vel = vel_local * lax.axis_size("vel")
    z_count = total_vel // (VXY * VXY)
    groups = send_list.shape[1]
    slot_count = send_list.shape[2]
    vel_index = lax.axis_index("vel") * vel_local + jnp.arange(vel_local, dtype=jnp.int32)
    velocity = velocity_nodes(vel_index, z_count)
    moment_table = moment_rows(velocity)
    quad_table = quad_rows(velocity).T
    is_local, source, slot_pos = ghost_slots(
        adjacency, block_counts[:, 0], cells, groups, slot_count
    )
    ghost_index = source * slot_count + slot_pos
    local_index = jnp.where(is_local, adjacency, 0)
    send_rows = send_list[0].reshape(-1)

    def reduce_moments(current):
        partial_value = (
            jnp.dot(
                moment_table,
                current,
                precision=lax.Precision.HIGHEST,
                preferred_element_type=jnp.float32,
            )
            / total_vel
        )
        return macroscopic(lax.psum(partial_value, "vel"))

    current = distribution
    for iteration in range(ITERS):
        params = reduce_moments(current)
        ghosts = lax.all_to_all(
            jnp.take(current, send_rows, axis=1), "space", split_axis=1, concat_axis=1, tiled=True
        )
        exponent = jnp.dot(
            quad_table,
            params[13:23],
            precision=lax.Precision.HIGHEST,
            preferred_element_type=jnp.float32,
        )
        equilibrium = jnp.exp(-0.5 * exponent)
        norm_z = lax.psum(jnp.sum(equilibrium, axis=0) / total_vel, "vel")
        neighbours = [
            jnp.where(
                is_local[side][None, :],
                jnp.take(current, local_index[side], axis=1),
                jnp.take(ghosts, ghost_index[side], axis=1),
            )
            for side in range(normals.shape[0])
        ]
        current = relax(current, neighbours, velocity, normals, params, norm_z, equilibrium)
    final = reduce_moments(current)
    return (current, final[:13])


MESH = pl.DeviceIdType.MESH
LOG2E = 1.4426950408889634
QUAD = 4
CHUNKS = 4
PIECES = 8
HELD = 3
HI = lax.Precision.HIGHEST


def coefficient_rows(m):
    full = macroscopic_rows(m)
    scale = -0.5 * LOG2E
    return full[:13], [row * scale for row in full[13:23]], full[23]


def macroscopic_rows(m):
    density = m[0]
    inv_d = 1.0 / density
    ux, uy, uz = (m[1] * inv_d, m[2] * inv_d, m[3] * inv_d)
    b = [m[r] * inv_d for r in range(4, 10)]
    third = [m[r] * inv_d for r in range(10, 13)]
    txx, tyy, tzz = (b[0] - ux * ux, b[1] - uy * uy, b[2] - uz * uz)
    txy, txz, tyz = (b[3] - ux * uy, b[4] - ux * uz, b[5] - uy * uz)
    temper = (txx + tyy + tzz) * (1.0 / 3.0)
    trace_b = b[0] + b[1] + b[2]
    bux = b[0] * ux + b[3] * uy + b[4] * uz
    buy = b[3] * ux + b[1] * uy + b[5] * uz
    buz = b[4] * ux + b[5] * uy + b[2] * uz
    usq = ux * ux + uy * uy + uz * uz
    qx = 0.5 * (third[0] - 2.0 * bux - ux * trace_b + 2.0 * ux * usq)
    qy = 0.5 * (third[1] - 2.0 * buy - uy * trace_b + 2.0 * uy * usq)
    qz = 0.5 * (third[2] - 2.0 * buz - uz * trace_b + 2.0 * uz * usq)
    iso = (1.0 - ellipsoid_mix) * temper
    lxx, lyy, lzz = (iso + ellipsoid_mix * txx, iso + ellipsoid_mix * tyy, iso + ellipsoid_mix * tzz)
    lxy, lxz, lyz = (ellipsoid_mix * txy, ellipsoid_mix * txz, ellipsoid_mix * tyz)
    cxx = lyy * lzz - lyz * lyz
    cxy = lyz * lxz - lxy * lzz
    cxz = lxy * lyz - lyy * lxz
    cyy = lxx * lzz - lxz * lxz
    cyz = lxy * lxz - lxx * lyz
    czz = lxx * lyy - lxy * lxy
    inv_det = 1.0 / (lxx * cxx + lxy * cxy + lxz * cxz)
    ixx, iyy, izz = (cxx * inv_det, cyy * inv_det, czz * inv_det)
    ixy, ixz, iyz = (cxy * inv_det, cxz * inv_det, cyz * inv_det)
    wx = ixx * ux + ixy * uy + ixz * uz
    wy = ixy * ux + iyy * uy + iyz * uz
    wz = ixz * ux + iyz * uy + izz * uz
    offset = ux * wx + uy * wy + uz * wz
    collide = prandtl * density * jnp.exp(visc_power * jnp.log(temper))
    return [
        density, ux, uy, uz, txx, tyy, tzz, txy, txz, tyz, qx, qy, qz,
        ixx, iyy, izz, 2.0 * ixy, 2.0 * ixz, 2.0 * iyz,
        -2.0 * wx, -2.0 * wy, -2.0 * wz, offset, collide,
    ]


def node_velocity(index, z_count):
    shift = VXY.bit_length() - 1
    centre = (VXY - 1) / 2.0
    vx = ((index & (VXY - 1)).astype(jnp.float32) - centre) * spacing
    vy = (((index >> shift) & (VXY - 1)).astype(jnp.float32) - centre) * spacing
    vz = ((index >> (2 * shift)).astype(jnp.float32) - (z_count - 1) / 2.0) * spacing
    return vx, vy, vz


def exponent_at(q, vx, vy, vz):
    return (
        vx * (q[0] * vx + q[3] * vy + q[4] * vz + q[6])
        + vy * (q[1] * vy + q[5] * vz + q[7])
        + (vz * (q[2] * vz + q[8]) + q[9])
    )


def x_column(width):
    rows = lax.broadcasted_iota(jnp.int32, (VXY, width), 0)
    return (rows.astype(jnp.float32) - (VXY - 1) / 2.0) * spacing


def gauss_total(q, width, z_count):
    vx = x_column(width)
    base = (q[0] * vx + q[6]) * vx

    def level(k, acc):
        vz = (k.astype(jnp.float32) - (z_count - 1) / 2.0) * spacing
        slope = q[4] * vz
        odd = q[5] * vz + q[7]
        even = vz * (q[2] * vz + q[8]) + q[9]
        level_base = base + vx * slope + even
        for j in range(VXY // 2):
            vy = (j + 0.5) * spacing
            mid = level_base + q[1] * (vy * vy)
            tilt = (vx * q[3] + odd) * vy
            acc = acc + (jnp.exp2(mid + tilt) + jnp.exp2(mid - tilt))
        return acc

    acc = lax.fori_loop(0, z_count, level, jnp.zeros((VXY, width), jnp.float32))
    return jnp.sum(acc, axis=0, keepdims=True)


def gauss_moments(q, width, z_count):
    vx = x_column(width)
    base = (q[0] * vx + q[6]) * vx
    zero = jnp.zeros((VXY, width), jnp.float32)

    def level(k, carry):
        vz = (k.astype(jnp.float32) - (z_count - 1) / 2.0) * spacing
        slope = q[4] * vz
        odd = q[5] * vz + q[7]
        even = vz * (q[2] * vz + q[8]) + q[9]
        level_base = base + vx * slope + even
        s0, s1, s2, s3 = (zero, zero, zero, zero)
        for j in range(VXY // 2):
            vy = (j + 0.5) * spacing
            mid = level_base + q[1] * (vy * vy)
            tilt = (vx * q[3] + odd) * vy
            up = jnp.exp2(mid + tilt)
            down = jnp.exp2(mid - tilt)
            both = up + down
            diff = (up - down) * vy
            s0 = s0 + both
            s1 = s1 + diff
            s2 = s2 + both * (vy * vy)
            s3 = s3 + diff * (vy * vy)
        z0 = vz * s0
        zz0 = vz * z0
        z1 = vz * s1
        new = (s0, s1, s2, s3, z0, zz0, z1, vz * zz0 + vz * s2, vz * z1)
        return tuple(a + b for a, b in zip(carry, new))

    s0, s1, s2, s3, z0, zz0, z1, zc, zz1 = lax.fori_loop(0, z_count, level, (zero,) * 9)
    vxx = vx * vx
    terms = [
        s0, vx * s0, s1, z0, vxx * s0, s2, zz0, vx * s1, vx * z0, z1,
        vx * (vxx * s0 + s2 + zz0), vxx * s1 + s3 + zz1, vxx * z0 + zc,
    ]
    return [jnp.sum(t, axis=0, keepdims=True) for t in terms]


def split_dot(lhs, rhs):
    return jnp.dot(lhs, rhs, precision=HI, preferred_element_type=jnp.float32)


def step_kernel(
    total_vel,
    f_hbm, n_ref, adj_ref, send_ref,
    out_hbm, fields_ref,
    f_ref, out_ref, load_s, store_s, fx, nx, adjx, sendx, oh, tr0, fnew, tr1, phi_ref,
    qb0, zb0, total_mine, total_theirs, qb1, zb1, qb2, zb2,
    bulk_s, bulk_r, meta_s, meta_r,
    a_s, a_r, b_s, b_r, x_s, x_r,
    d_s, d_r, e_s, e_r, g_s, g_r, h_s, h_r,
):
    nodes, cells = f_hbm.shape
    both = 2 * cells
    faces = n_ref.shape[1]
    z_count = total_vel // (VXY * VXY)
    rows = nodes // CHUNKS
    group = lax.axis_index("space")
    other = 1 - group
    vel = lax.axis_index("vel")
    ring = total_vel // nodes // QUAD
    me_q = lax.rem(vel, QUAD)
    me_z = vel // QUAD

    def at(space, z, q):
        return (space, z * QUAD + q)

    def q_of(step):
        return lax.rem(me_q + step, QUAD)

    def z_of(step):
        return lax.rem(me_z + step, ring)

    barrier = pltpu.get_barrier_semaphore()
    for step in range(1, QUAD):
        pl.semaphore_signal(barrier, inc=1, device_id=at(group, me_z, q_of(step)), device_id_type=MESH)
    for step in range(1, ring):
        pl.semaphore_signal(barrier, inc=1, device_id=at(group, z_of(step), me_q), device_id_type=MESH)
    pl.semaphore_signal(barrier, inc=1, device_id=at(other, me_z, me_q), device_id_type=MESH)

    load = pltpu.make_async_copy(f_hbm, f_ref, load_s)
    load.start()

    lane_v = node_velocity(lax.broadcasted_iota(jnp.int32, (1, nodes), 1) + vel * nodes, z_count)
    lx, ly, lz = lane_v
    sq = lx * lx + ly * ly + lz * lz
    table = [
        jnp.ones_like(lx), lx, ly, lz, lx * lx, ly * ly, lz * lz,
        lx * ly, lx * lz, ly * lz, lx * sq, ly * sq, lz * sq,
    ]
    row_id = lax.broadcasted_iota(jnp.int32, (16, nodes), 0)
    phi = jnp.zeros((16, nodes), jnp.float32)
    for r, row in enumerate(table):
        phi = jnp.where(row_id == r, row, phi)
    phi_ref[...] = phi
    inv_total = 1.0 / total_vel
    load.wait()
    qb0[me_q] = split_dot(phi, f_ref[...]) * inv_total

    pl.semaphore_wait(barrier, QUAD + ring - 1)

    def remote(src, dst, s, r, dev):
        return pltpu.make_async_remote_copy(
            src_ref=src, dst_ref=dst, send_sem=s, recv_sem=r, device_id=dev, device_id_type=MESH
        )

    pair = at(other, me_z, me_q)
    metas = [
        remote(send_ref, sendx, meta_s.at[0], meta_r.at[0], pair),
        remote(adj_ref, adjx, meta_s.at[1], meta_r.at[1], pair),
        remote(n_ref, nx, meta_s.at[2], meta_r.at[2], pair),
    ]
    for copy in metas:
        copy.start()

    def in_quad(buffer, s, r):
        copies = [
            remote(buffer.at[me_q], buffer.at[me_q], s.at[t], r.at[t], at(group, me_z, q_of(t)))
            for t in range(1, QUAD)
        ]
        for copy in copies:
            copy.start()
        return copies

    def along_z(buffer, s, r):
        copies = [
            remote(buffer.at[me_z], buffer.at[me_z], s.at[t], r.at[t], at(group, z_of(t), me_q))
            for t in range(1, ring)
        ]
        for copy in copies:
            copy.start()
        return copies

    def collect(copies, buffer, count):
        for copy in copies:
            copy.wait_recv()
        result = buffer[0]
        for t in range(1, count):
            result = result + buffer[t]
        return result

    piece = nodes // PIECES
    ratio = PIECES // CHUNKS

    def bulk(c):
        part = pl.ds(pl.multiple_of(c * piece, piece), piece)
        return remote(f_ref.at[part], fx.at[part], bulk_s.at[c], bulk_r.at[c], pair)

    first = in_quad(qb0, a_s, a_r)
    for c in range(PIECES - HELD):
        bulk(c).start()

    for copy in metas:
        copy.wait_recv()
    slot_id = lax.broadcasted_iota(jnp.int32, (cells, cells), 0)
    cell_id = lax.broadcasted_iota(jnp.int32, (both, both), 0)

    def listed(send_row, adjacency):
        hit = (slot_id == adjacency - cells).astype(jnp.bfloat16)
        values = jnp.broadcast_to(send_row, (8, cells)).astype(jnp.float32).astype(jnp.bfloat16)
        got = jnp.dot(values, hit, preferred_element_type=jnp.float32)
        return got[0:1].astype(jnp.int32)

    to_me = sendx[0, pl.ds(group, 1), :]
    to_other = send_ref[0, pl.ds(other, 1), :]
    for k in range(faces):
        own = adj_ref[k : k + 1, :]
        theirs = adjx[k : k + 1, :]
        own = jnp.where(own < cells, own, cells + listed(to_me, own))
        theirs = jnp.where(theirs < cells, cells + theirs, listed(to_other, theirs))
        index = jnp.concatenate([own, theirs], axis=1)
        oh[k] = (cell_id == index).astype(jnp.bfloat16)

    zb0[me_z] = collect(first, qb0, QUAD)
    second = along_z(zb0, b_s, b_r)

    def local_velocity(c, width):
        index = lax.broadcasted_iota(jnp.int32, (rows, width), 0) + (vel * nodes + c * rows)
        return node_velocity(index, z_count)

    def transport(state, c, width):
        high = state.astype(jnp.bfloat16)
        low = (state - high.astype(jnp.float32)).astype(jnp.bfloat16)
        lhs = jnp.concatenate([high, low], axis=0)
        vx, vy, vz = local_velocity(c, width)
        mine = state[:, :width]
        result = jnp.zeros((rows, width), jnp.float32)
        for k in range(faces):
            got = jnp.dot(lhs, oh[k, :, 0:width], preferred_element_type=jnp.float32)
            got = got[:rows] + got[rows:]
            normal = []
            for d in range(3):
                line = n_ref[d, k : k + 1, :]
                if width > cells:
                    line = jnp.concatenate([line, nx[d, k : k + 1, :]], axis=1)
                normal.append(line)
            speed = vx * normal[0] + vy * normal[1] + vz * normal[2]
            result = result + (jnp.maximum(speed, 0.0) * mine + jnp.minimum(speed, 0.0) * got)
        return result

    def wide(c):
        part = pl.ds(pl.multiple_of(c * rows, rows), rows)
        return part, jnp.concatenate([f_ref[part, :], fx[part, :]], axis=1)

    def first_transport(c, carry):
        for t in range(ratio):
            bulk(c * ratio + t).wait_recv()
        part, state = wide(c)
        tr0[part, :] = transport(state, c, both)
        return carry

    lax.fori_loop(0, CHUNKS // 2, first_transport, 0)
    total_mine[...] = collect(second, zb0, ring)
    third = [remote(total_mine, total_theirs, x_s, x_r, pair)]
    third[0].start()
    for c in range(PIECES - HELD, PIECES):
        bulk(c).start()

    def rows_of(moments):
        return [moments[r : r + 1] for r in range(13)]

    mom0 = rows_of(total_mine[...])
    fields0, own_quad, freq0 = coefficient_rows(mom0)
    sums0 = gauss_moments(own_quad, cells, z_count)
    lift0 = time_step * freq0 * fields0[0] / sums0[0]
    own_gain = lift0 * float(total_vel)
    own_keep = 1.0 - time_step * freq0
    lax.fori_loop(CHUNKS // 2, CHUNKS - 1, first_transport, 0)
    third[0].wait_recv()
    fields_x, their_quad, freq_x = coefficient_rows(rows_of(total_theirs[...]))
    norm_x = gauss_total(their_quad, cells, z_count) * inv_total
    their_gain = time_step * freq_x * fields_x[0] / norm_x
    their_keep = 1.0 - time_step * freq_x
    quad0 = [jnp.concatenate([a, b], axis=1) for a, b in zip(own_quad, their_quad)]
    gain0 = jnp.concatenate([own_gain, their_gain], axis=1)
    keep0 = jnp.concatenate([own_keep, their_keep], axis=1)
    ahead = nodes - rows
    phi = phi_ref[...]
    m_t0 = split_dot(phi[:, :ahead], tr0[:ahead, :cells])
    lax.fori_loop(CHUNKS - 1, CHUNKS, first_transport, 0)
    qb1[me_q] = (m_t0 + split_dot(phi[:, ahead:], tr0[ahead:, :cells])) * inv_total
    fourth = in_quad(qb1, d_s, d_r)

    def second_transport(c, carry):
        part, state = wide(c)
        vx, vy, vz = local_velocity(c, both)
        state = keep0 * state - time_step * tr0[part, :] + gain0 * jnp.exp2(exponent_at(quad0, vx, vy, vz))
        fnew[part, :] = state[:, :cells]
        tr1[part, :] = transport(state, c, cells)
        return carry

    lax.fori_loop(0, CHUNKS // 2, second_transport, 0)
    zb1[me_z] = collect(fourth, qb1, QUAD)
    sixth = along_z(zb1, g_s, g_r)
    lax.fori_loop(CHUNKS // 2, CHUNKS, second_transport, 0)
    qb2[me_q] = split_dot(phi, tr1[...]) * inv_total
    fifth = in_quad(qb2, e_s, e_r)
    zb2[me_z] = collect(fifth, qb2, QUAD)
    seventh = along_z(zb2, h_s, h_r)
    mom_t0 = collect(sixth, zb1, ring)
    mom1 = [
        own_keep * mom0[r] - time_step * mom_t0[r : r + 1] + lift0 * sums0[r] for r in range(13)
    ]
    fields1, quad1, freq1 = coefficient_rows(mom1)
    sums = gauss_moments(quad1, cells, z_count)
    inv_sum = 1.0 / sums[0]
    lift = time_step * freq1 * fields1[0]
    gain1 = lift * inv_sum * float(total_vel)
    keep1 = 1.0 - time_step * freq1

    def store(c):
        part = pl.ds(pl.multiple_of(c * rows, rows), rows)
        return pltpu.make_async_copy(out_ref.at[part], out_hbm.at[part], store_s.at[c])

    def finish(c, carry):
        part = pl.ds(pl.multiple_of(c * rows, rows), rows)
        vx, vy, vz = local_velocity(c, cells)
        out_ref[part, :] = (
            keep1 * fnew[part, :] - time_step * tr1[part, :]
            + gain1 * jnp.exp2(exponent_at(quad1, vx, vy, vz))
        )
        store(c).start()
        return carry

    lax.fori_loop(0, CHUNKS, finish, 0)
    mom_t = collect(seventh, zb2, ring)
    slope = lift * inv_sum
    last = [
        keep1 * mom1[r] - time_step * mom_t[r : r + 1] + slope * sums[r] for r in range(13)
    ]
    final = macroscopic_rows(last)
    for r in range(13):
        fields_ref[r : r + 1, :] = final[r]
    for c in range(CHUNKS):
        store(c).wait()
    for c in range(PIECES):
        bulk(c).wait_send()
    for copy in metas + first + second + third + fourth + fifth + sixth + seventh:
        copy.wait_send()


def per_device_pair(distribution, normals, adjacency, send_list, block_counts):
    nodes, cells = distribution.shape
    normals = normals.transpose(1, 0, 2)
    size = lax.axis_size("vel")
    ring = size // QUAD
    f32 = jnp.float32
    dma = pltpu.SemaphoreType.DMA
    vmem = pl.BlockSpec(memory_space=pltpu.VMEM)
    anywhere = pl.BlockSpec(memory_space=pl.ANY)
    return pl.pallas_call(
        functools.partial(step_kernel, nodes * size),
        out_shape=(
            jax.ShapeDtypeStruct((nodes, cells), f32),
            jax.ShapeDtypeStruct((13, cells), f32),
        ),
        in_specs=[anywhere] + [vmem] * 3,
        out_specs=(anywhere, vmem),
        scratch_shapes=[
            pltpu.VMEM((nodes, cells), f32),
            pltpu.VMEM((nodes, cells), f32),
            dma,
            dma((CHUNKS,)),
            pltpu.VMEM((nodes, cells), f32),
            pltpu.VMEM(normals.shape, f32),
            pltpu.VMEM(adjacency.shape, jnp.int32),
            pltpu.VMEM(send_list.shape, jnp.int32),
            pltpu.VMEM((normals.shape[1], 2 * cells, 2 * cells), jnp.bfloat16),
            pltpu.VMEM((nodes, 2 * cells), f32),
            pltpu.VMEM((nodes, cells), f32),
            pltpu.VMEM((nodes, cells), f32),
            pltpu.VMEM((16, nodes), f32),
            pltpu.VMEM((QUAD, 16, cells), f32),
            pltpu.VMEM((ring, 16, cells), f32),
            pltpu.VMEM((16, cells), f32),
            pltpu.VMEM((16, cells), f32),
            pltpu.VMEM((QUAD, 16, cells), f32),
            pltpu.VMEM((ring, 16, cells), f32),
            pltpu.VMEM((QUAD, 16, cells), f32),
            pltpu.VMEM((ring, 16, cells), f32),
            dma((PIECES,)), dma((PIECES,)), dma((3,)), dma((3,)),
            dma((QUAD,)), dma((QUAD,)), dma((ring,)), dma((ring,)), dma, dma,
            dma((QUAD,)), dma((QUAD,)), dma((QUAD,)), dma((QUAD,)),
            dma((ring,)), dma((ring,)), dma((ring,)), dma((ring,)),
        ],
        compiler_params=pltpu.CompilerParams(collective_id=0, has_side_effects=True),
        name="steps",
    )(distribution, normals, adjacency, send_list)


def solution(mesh):
    placed = (
        P("vel", "space"),
        P(None, None, "space"),
        P(None, "space"),
        P("space", None, None),
        P(None, "space"),
    )
    pair = mesh.shape["space"] == 2 and mesh.shape["vel"] % QUAD == 0 and ITERS == 2
    return jax.shard_map(
        per_device_pair if pair else per_device,
        mesh=mesh,
        in_specs=placed,
        out_specs=(P("vel", "space"), P(None, "space")),
        check_vma=False,
    )
```

```python
import functools

import jax
import jax.numpy as jnp
from jax import lax
from jax.experimental import pallas as pl
from jax.experimental.pallas import tpu as pltpu
from jax.sharding import PartitionSpec as P

VXY = 32
TILE = 128
ITERS = 2


spacing = 0.3
ellipsoid_mix = -0.25
prandtl = 0.8
visc_power = 0.26
time_step = 0.025


def velocity_nodes(vel_index, z_count):
    comp_x = (vel_index % VXY).astype(jnp.float32)
    comp_y = (vel_index // VXY % VXY).astype(jnp.float32)
    comp_z = (vel_index // (VXY * VXY)).astype(jnp.float32)
    centre = (VXY - 1) / 2.0
    return jnp.stack(
        [
            (comp_x - centre) * spacing,
            (comp_y - centre) * spacing,
            (comp_z - (z_count - 1) / 2.0) * spacing,
        ]
    )


def moment_rows(velocity):
    comp_x, comp_y, comp_z = (velocity[0], velocity[1], velocity[2])
    squared = comp_x * comp_x + comp_y * comp_y + comp_z * comp_z
    return jnp.stack(
        [
            jnp.ones_like(comp_x),
            comp_x,
            comp_y,
            comp_z,
            comp_x * comp_x,
            comp_y * comp_y,
            comp_z * comp_z,
            comp_x * comp_y,
            comp_x * comp_z,
            comp_y * comp_z,
            comp_x * squared,
            comp_y * squared,
            comp_z * squared,
        ]
    )


def quad_rows(velocity):
    comp_x, comp_y, comp_z = (velocity[0], velocity[1], velocity[2])
    return jnp.stack(
        [
            comp_x * comp_x,
            comp_y * comp_y,
            comp_z * comp_z,
            comp_x * comp_y,
            comp_x * comp_z,
            comp_y * comp_z,
            comp_x,
            comp_y,
            comp_z,
            jnp.ones_like(comp_x),
        ]
    )


def macroscopic(moments):
    density = moments[0]
    mean_x = moments[1] / density
    mean_y = moments[2] / density
    mean_z = moments[3] / density
    second = moments[4:10] / density[None, :]
    third = moments[10:13] / density[None, :]
    theta_xx = second[0] - mean_x * mean_x
    theta_yy = second[1] - mean_y * mean_y
    theta_zz = second[2] - mean_z * mean_z
    theta_xy = second[3] - mean_x * mean_y
    theta_xz = second[4] - mean_x * mean_z
    theta_yz = second[5] - mean_y * mean_z
    temper = (theta_xx + theta_yy + theta_zz) / 3.0
    trace_b = second[0] + second[1] + second[2]
    bu_x = second[0] * mean_x + second[3] * mean_y + second[4] * mean_z
    bu_y = second[3] * mean_x + second[1] * mean_y + second[5] * mean_z
    bu_z = second[4] * mean_x + second[5] * mean_y + second[2] * mean_z
    mean_sq = mean_x * mean_x + mean_y * mean_y + mean_z * mean_z
    flux_x = 0.5 * (third[0] - 2.0 * bu_x - mean_x * trace_b + 2.0 * mean_x * mean_sq)
    flux_y = 0.5 * (third[1] - 2.0 * bu_y - mean_y * trace_b + 2.0 * mean_y * mean_sq)
    flux_z = 0.5 * (third[2] - 2.0 * bu_z - mean_z * trace_b + 2.0 * mean_z * mean_sq)
    iso_part = (1.0 - ellipsoid_mix) * temper
    lam_xx = iso_part + ellipsoid_mix * theta_xx
    lam_yy = iso_part + ellipsoid_mix * theta_yy
    lam_zz = iso_part + ellipsoid_mix * theta_zz
    lam_xy = ellipsoid_mix * theta_xy
    lam_xz = ellipsoid_mix * theta_xz
    lam_yz = ellipsoid_mix * theta_yz
    cof_xx = lam_yy * lam_zz - lam_yz * lam_yz
    cof_xy = lam_yz * lam_xz - lam_xy * lam_zz
    cof_xz = lam_xy * lam_yz - lam_yy * lam_xz
    cof_yy = lam_xx * lam_zz - lam_xz * lam_xz
    cof_yz = lam_xy * lam_xz - lam_xx * lam_yz
    cof_zz = lam_xx * lam_yy - lam_xy * lam_xy
    determinant = lam_xx * cof_xx + lam_xy * cof_xy + lam_xz * cof_xz
    inv_xx = cof_xx / determinant
    inv_yy = cof_yy / determinant
    inv_zz = cof_zz / determinant
    inv_xy = cof_xy / determinant
    inv_xz = cof_xz / determinant
    inv_yz = cof_yz / determinant
    lin_x = inv_xx * mean_x + inv_xy * mean_y + inv_xz * mean_z
    lin_y = inv_xy * mean_x + inv_yy * mean_y + inv_yz * mean_z
    lin_z = inv_xz * mean_x + inv_yz * mean_y + inv_zz * mean_z
    offset = mean_x * lin_x + mean_y * lin_y + mean_z * lin_z
    collide = prandtl * density * jnp.exp(visc_power * jnp.log(temper))
    return jnp.stack(
        [
            density,
            mean_x,
            mean_y,
            mean_z,
            theta_xx,
            theta_yy,
            theta_zz,
            theta_xy,
            theta_xz,
            theta_yz,
            flux_x,
            flux_y,
            flux_z,
            inv_xx,
            inv_yy,
            inv_zz,
            2.0 * inv_xy,
            2.0 * inv_xz,
            2.0 * inv_yz,
            -2.0 * lin_x,
            -2.0 * lin_y,
            -2.0 * lin_z,
            offset,
            collide,
        ]
    )


def ghost_slots(adjacency, counts, cells, groups, slot_count):
    ends = jnp.cumsum(counts) * TILE
    starts = ends - counts * TILE
    is_local = adjacency < cells
    position = jnp.maximum(adjacency - cells, 0)
    source = jnp.sum((ends[:, None, None] <= position[None]).astype(jnp.int32), axis=0)
    source = jnp.minimum(source, groups - 1)
    group_ids = jnp.arange(groups, dtype=jnp.int32)[:, None, None]
    chosen = jnp.sum(jnp.where(group_ids == source[None], starts[:, None, None], 0), axis=0)
    slot_pos = jnp.clip(position - chosen, 0, slot_count - 1)
    return (is_local, source, slot_pos)


def relax(current, neighbours, velocity, normals, params, norm_z, equilibrium):
    gauss = params[0][None, :] * equilibrium / norm_z[None, :]
    outflow = jnp.zeros(current.shape, jnp.float32)
    inflow = jnp.zeros(current.shape, jnp.float32)
    for side in range(normals.shape[0]):
        normal_speed = (
            velocity[0][:, None] * normals[side, 0][None, :]
            + velocity[1][:, None] * normals[side, 1][None, :]
            + velocity[2][:, None] * normals[side, 2][None, :]
        )
        outflow = outflow + jnp.maximum(normal_speed, 0.0)
        inflow = inflow + jnp.minimum(normal_speed, 0.0) * neighbours[side]
    return current + time_step * (
        params[23][None, :] * (gauss - current) - outflow * current - inflow
    )


def per_device(distribution, normals, adjacency, send_list, block_counts):
    vel_local = distribution.shape[0]
    cells = distribution.shape[1]
    total_vel = vel_local * lax.axis_size("vel")
    z_count = total_vel // (VXY * VXY)
    groups = send_list.shape[1]
    slot_count = send_list.shape[2]
    vel_index = lax.axis_index("vel") * vel_local + jnp.arange(vel_local, dtype=jnp.int32)
    velocity = velocity_nodes(vel_index, z_count)
    moment_table = moment_rows(velocity)
    quad_table = quad_rows(velocity).T
    is_local, source, slot_pos = ghost_slots(
        adjacency, block_counts[:, 0], cells, groups, slot_count
    )
    ghost_index = source * slot_count + slot_pos
    local_index = jnp.where(is_local, adjacency, 0)
    send_rows = send_list[0].reshape(-1)

    def reduce_moments(current):
        partial_value = (
            jnp.dot(
                moment_table,
                current,
                precision=lax.Precision.HIGHEST,
                preferred_element_type=jnp.float32,
            )
            / total_vel
        )
        return macroscopic(lax.psum(partial_value, "vel"))

    current = distribution
    for iteration in range(ITERS):
        params = reduce_moments(current)
        ghosts = lax.all_to_all(
            jnp.take(current, send_rows, axis=1), "space", split_axis=1, concat_axis=1, tiled=True
        )
        exponent = jnp.dot(
            quad_table,
            params[13:23],
            precision=lax.Precision.HIGHEST,
            preferred_element_type=jnp.float32,
        )
        equilibrium = jnp.exp(-0.5 * exponent)
        norm_z = lax.psum(jnp.sum(equilibrium, axis=0) / total_vel, "vel")
        neighbours = [
            jnp.where(
                is_local[side][None, :],
                jnp.take(current, local_index[side], axis=1),
                jnp.take(ghosts, ghost_index[side], axis=1),
            )
            for side in range(normals.shape[0])
        ]
        current = relax(current, neighbours, velocity, normals, params, norm_z, equilibrium)
    final = reduce_moments(current)
    return (current, final[:13])


MESH = pl.DeviceIdType.MESH
LOG2E = 1.4426950408889634
QUAD = 4
CHUNKS = 4
PIECES = 8
HELD = 3
HI = lax.Precision.HIGHEST


def coefficient_rows(m):
    full = macroscopic_rows(m)
    scale = -0.5 * LOG2E
    return full[:13], [row * scale for row in full[13:23]], full[23]


def macroscopic_rows(m):
    density = m[0]
    inv_d = 1.0 / density
    ux, uy, uz = (m[1] * inv_d, m[2] * inv_d, m[3] * inv_d)
    b = [m[r] * inv_d for r in range(4, 10)]
    third = [m[r] * inv_d for r in range(10, 13)]
    txx, tyy, tzz = (b[0] - ux * ux, b[1] - uy * uy, b[2] - uz * uz)
    txy, txz, tyz = (b[3] - ux * uy, b[4] - ux * uz, b[5] - uy * uz)
    temper = (txx + tyy + tzz) * (1.0 / 3.0)
    trace_b = b[0] + b[1] + b[2]
    bux = b[0] * ux + b[3] * uy + b[4] * uz
    buy = b[3] * ux + b[1] * uy + b[5] * uz
    buz = b[4] * ux + b[5] * uy + b[2] * uz
    usq = ux * ux + uy * uy + uz * uz
    qx = 0.5 * (third[0] - 2.0 * bux - ux * trace_b + 2.0 * ux * usq)
    qy = 0.5 * (third[1] - 2.0 * buy - uy * trace_b + 2.0 * uy * usq)
    qz = 0.5 * (third[2] - 2.0 * buz - uz * trace_b + 2.0 * uz * usq)
    iso = (1.0 - ellipsoid_mix) * temper
    lxx, lyy, lzz = (iso + ellipsoid_mix * txx, iso + ellipsoid_mix * tyy, iso + ellipsoid_mix * tzz)
    lxy, lxz, lyz = (ellipsoid_mix * txy, ellipsoid_mix * txz, ellipsoid_mix * tyz)
    cxx = lyy * lzz - lyz * lyz
    cxy = lyz * lxz - lxy * lzz
    cxz = lxy * lyz - lyy * lxz
    cyy = lxx * lzz - lxz * lxz
    cyz = lxy * lxz - lxx * lyz
    czz = lxx * lyy - lxy * lxy
    inv_det = 1.0 / (lxx * cxx + lxy * cxy + lxz * cxz)
    ixx, iyy, izz = (cxx * inv_det, cyy * inv_det, czz * inv_det)
    ixy, ixz, iyz = (cxy * inv_det, cxz * inv_det, cyz * inv_det)
    wx = ixx * ux + ixy * uy + ixz * uz
    wy = ixy * ux + iyy * uy + iyz * uz
    wz = ixz * ux + iyz * uy + izz * uz
    offset = ux * wx + uy * wy + uz * wz
    collide = prandtl * density * jnp.exp(visc_power * jnp.log(temper))
    return [
        density, ux, uy, uz, txx, tyy, tzz, txy, txz, tyz, qx, qy, qz,
        ixx, iyy, izz, 2.0 * ixy, 2.0 * ixz, 2.0 * iyz,
        -2.0 * wx, -2.0 * wy, -2.0 * wz, offset, collide,
    ]


def node_velocity(index, z_count):
    shift = VXY.bit_length() - 1
    centre = (VXY - 1) / 2.0
    vx = ((index & (VXY - 1)).astype(jnp.float32) - centre) * spacing
    vy = (((index >> shift) & (VXY - 1)).astype(jnp.float32) - centre) * spacing
    vz = ((index >> (2 * shift)).astype(jnp.float32) - (z_count - 1) / 2.0) * spacing
    return vx, vy, vz


def exponent_at(q, vx, vy, vz):
    return (
        vx * (q[0] * vx + q[3] * vy + q[4] * vz + q[6])
        + vy * (q[1] * vy + q[5] * vz + q[7])
        + (vz * (q[2] * vz + q[8]) + q[9])
    )


def x_column(width):
    rows = lax.broadcasted_iota(jnp.int32, (VXY, width), 0)
    return (rows.astype(jnp.float32) - (VXY - 1) / 2.0) * spacing


def gauss_total(q, width, z_count):
    vx = x_column(width)
    base = (q[0] * vx + q[6]) * vx

    def level(k, acc):
        vz = (k.astype(jnp.float32) - (z_count - 1) / 2.0) * spacing
        slope = q[4] * vz
        odd = q[5] * vz + q[7]
        even = vz * (q[2] * vz + q[8]) + q[9]
        level_base = base + vx * slope + even
        for j in range(VXY // 2):
            vy = (j + 0.5) * spacing
            mid = level_base + q[1] * (vy * vy)
            tilt = (vx * q[3] + odd) * vy
            acc = acc + (jnp.exp2(mid + tilt) + jnp.exp2(mid - tilt))
        return acc

    acc = lax.fori_loop(0, z_count, level, jnp.zeros((VXY, width), jnp.float32))
    return jnp.sum(acc, axis=0, keepdims=True)


def gauss_moments(q, width, z_count):
    vx = x_column(width)
    base = (q[0] * vx + q[6]) * vx
    zero = jnp.zeros((VXY, width), jnp.float32)

    def level(k, carry):
        vz = (k.astype(jnp.float32) - (z_count - 1) / 2.0) * spacing
        slope = q[4] * vz
        odd = q[5] * vz + q[7]
        even = vz * (q[2] * vz + q[8]) + q[9]
        level_base = base + vx * slope + even
        s0, s1, s2, s3 = (zero, zero, zero, zero)
        for j in range(VXY // 2):
            vy = (j + 0.5) * spacing
            mid = level_base + q[1] * (vy * vy)
            tilt = (vx * q[3] + odd) * vy
            up = jnp.exp2(mid + tilt)
            down = jnp.exp2(mid - tilt)
            both = up + down
            diff = (up - down) * vy
            s0 = s0 + both
            s1 = s1 + diff
            s2 = s2 + both * (vy * vy)
            s3 = s3 + diff * (vy * vy)
        z0 = vz * s0
        zz0 = vz * z0
        z1 = vz * s1
        new = (s0, s1, s2, s3, z0, zz0, z1, vz * zz0 + vz * s2, vz * z1)
        return tuple(a + b for a, b in zip(carry, new))

    s0, s1, s2, s3, z0, zz0, z1, zc, zz1 = lax.fori_loop(0, z_count, level, (zero,) * 9)
    vxx = vx * vx
    terms = [
        s0, vx * s0, s1, z0, vxx * s0, s2, zz0, vx * s1, vx * z0, z1,
        vx * (vxx * s0 + s2 + zz0), vxx * s1 + s3 + zz1, vxx * z0 + zc,
    ]
    return [jnp.sum(t, axis=0, keepdims=True) for t in terms]


def split_dot(lhs, rhs):
    return jnp.dot(lhs, rhs, precision=HI, preferred_element_type=jnp.float32)


def step_kernel(
    total_vel,
    f_hbm, n_ref, adj_ref, send_ref,
    out_hbm, fields_ref,
    f_ref, out_ref, load_s, store_s, fx, nx, adjx, sendx, oh, tr0, fnew, tr1, phi_ref,
    qb0, zb0, total_mine, total_theirs, qb1, zb1, qb2, zb2,
    bulk_s, bulk_r, meta_s, meta_r,
    a_s, a_r, b_s, b_r, x_s, x_r,
    d_s, d_r, e_s, e_r, g_s, g_r, h_s, h_r,
):
    nodes, cells = f_hbm.shape
    both = 2 * cells
    faces = n_ref.shape[1]
    z_count = total_vel // (VXY * VXY)
    rows = nodes // CHUNKS
    group = lax.axis_index("space")
    other = 1 - group
    vel = lax.axis_index("vel")
    ring = total_vel // nodes // QUAD
    me_q = lax.rem(vel, QUAD)
    me_z = vel // QUAD

    def at(space, z, q):
        return (space, z * QUAD + q)

    def q_of(step):
        return lax.rem(me_q + step, QUAD)

    def z_of(step):
        return lax.rem(me_z + step, ring)

    barrier = pltpu.get_barrier_semaphore()
    for step in range(1, QUAD):
        pl.semaphore_signal(barrier, inc=1, device_id=at(group, me_z, q_of(step)), device_id_type=MESH)
    for step in range(1, ring):
        pl.semaphore_signal(barrier, inc=1, device_id=at(group, z_of(step), me_q), device_id_type=MESH)
    pl.semaphore_signal(barrier, inc=1, device_id=at(other, me_z, me_q), device_id_type=MESH)

    load = pltpu.make_async_copy(f_hbm, f_ref, load_s)
    load.start()

    lane_v = node_velocity(lax.broadcasted_iota(jnp.int32, (1, nodes), 1) + vel * nodes, z_count)
    lx, ly, lz = lane_v
    sq = lx * lx + ly * ly + lz * lz
    table = [
        jnp.ones_like(lx), lx, ly, lz, lx * lx, ly * ly, lz * lz,
        lx * ly, lx * lz, ly * lz, lx * sq, ly * sq, lz * sq,
    ]
    row_id = lax.broadcasted_iota(jnp.int32, (16, nodes), 0)
    phi = jnp.zeros((16, nodes), jnp.float32)
    for r, row in enumerate(table):
        phi = jnp.where(row_id == r, row, phi)
    phi_ref[...] = phi
    inv_total = 1.0 / total_vel
    load.wait()
    qb0[me_q] = split_dot(phi, f_ref[...]) * inv_total

    pl.semaphore_wait(barrier, QUAD + ring - 1)

    def remote(src, dst, s, r, dev):
        return pltpu.make_async_remote_copy(
            src_ref=src, dst_ref=dst, send_sem=s, recv_sem=r, device_id=dev, device_id_type=MESH
        )

    pair = at(other, me_z, me_q)
    metas = [
        remote(send_ref, sendx, meta_s.at[0], meta_r.at[0], pair),
        remote(adj_ref, adjx, meta_s.at[1], meta_r.at[1], pair),
        remote(n_ref, nx, meta_s.at[2], meta_r.at[2], pair),
    ]
    for copy in metas:
        copy.start()

    def in_quad(buffer, s, r):
        copies = [
            remote(buffer.at[me_q], buffer.at[me_q], s.at[t], r.at[t], at(group, me_z, q_of(t)))
            for t in range(1, QUAD)
        ]
        for copy in copies:
            copy.start()
        return copies

    def along_z(buffer, s, r):
        copies = [
            remote(buffer.at[me_z], buffer.at[me_z], s.at[t], r.at[t], at(group, z_of(t), me_q))
            for t in range(1, ring)
        ]
        for copy in copies:
            copy.start()
        return copies

    def collect(copies, buffer, count):
        for copy in copies:
            copy.wait_recv()
        result = buffer[0]
        for t in range(1, count):
            result = result + buffer[t]
        return result

    piece = nodes // PIECES
    ratio = PIECES // CHUNKS

    def bulk(c):
        part = pl.ds(pl.multiple_of(c * piece, piece), piece)
        return remote(f_ref.at[part], fx.at[part], bulk_s.at[c], bulk_r.at[c], pair)

    first = in_quad(qb0, a_s, a_r)
    for c in range(PIECES - HELD):
        bulk(c).start()

    for copy in metas:
        copy.wait_recv()
    slot_id = lax.broadcasted_iota(jnp.int32, (cells, cells), 0)
    cell_id = lax.broadcasted_iota(jnp.int32, (both, both), 0)

    def listed(send_row, adjacency):
        hit = (slot_id == adjacency - cells).astype(jnp.bfloat16)
        values = jnp.broadcast_to(send_row, (8, cells)).astype(jnp.float32).astype(jnp.bfloat16)
        got = jnp.dot(values, hit, preferred_element_type=jnp.float32)
        return got[0:1].astype(jnp.int32)

    to_me = sendx[0, pl.ds(group, 1), :]
    to_other = send_ref[0, pl.ds(other, 1), :]
    for k in range(faces):
        own = adj_ref[k : k + 1, :]
        theirs = adjx[k : k + 1, :]
        own = jnp.where(own < cells, own, cells + listed(to_me, own))
        theirs = jnp.where(theirs < cells, cells + theirs, listed(to_other, theirs))
        index = jnp.concatenate([own, theirs], axis=1)
        oh[k] = (cell_id == index).astype(jnp.bfloat16)

    zb0[me_z] = collect(first, qb0, QUAD)
    second = along_z(zb0, b_s, b_r)

    def local_velocity(c, width):
        index = lax.broadcasted_iota(jnp.int32, (rows, width), 0) + (vel * nodes + c * rows)
        return node_velocity(index, z_count)

    def transport(state, c, width):
        high = state.astype(jnp.bfloat16)
        low = (state - high.astype(jnp.float32)).astype(jnp.bfloat16)
        lhs = jnp.concatenate([high, low], axis=0)
        vx, vy, vz = local_velocity(c, width)
        mine = state[:, :width]
        result = jnp.zeros((rows, width), jnp.float32)
        for k in range(faces):
            got = jnp.dot(lhs, oh[k, :, 0:width], preferred_element_type=jnp.float32)
            got = got[:rows] + got[rows:]
            normal = []
            for d in range(3):
                line = n_ref[d, k : k + 1, :]
                if width > cells:
                    line = jnp.concatenate([line, nx[d, k : k + 1, :]], axis=1)
                normal.append(line)
            speed = vx * normal[0] + vy * normal[1] + vz * normal[2]
            result = result + (jnp.maximum(speed, 0.0) * mine + jnp.minimum(speed, 0.0) * got)
        return result

    def wide(c):
        part = pl.ds(pl.multiple_of(c * rows, rows), rows)
        return part, jnp.concatenate([f_ref[part, :], fx[part, :]], axis=1)

    def first_transport(c, carry):
        for t in range(ratio):
            bulk(c * ratio + t).wait_recv()
        part, state = wide(c)
        tr0[part, :] = transport(state, c, both)
        return carry

    lax.fori_loop(0, 1, first_transport, 0)
    total_mine[...] = collect(second, zb0, ring)
    third = [remote(total_mine, total_theirs, x_s, x_r, pair)]
    third[0].start()
    for c in range(PIECES - HELD, PIECES):
        bulk(c).start()

    def rows_of(moments):
        return [moments[r : r + 1] for r in range(13)]

    mom0 = rows_of(total_mine[...])
    fields0, own_quad, freq0 = coefficient_rows(mom0)
    sums0 = gauss_moments(own_quad, cells, z_count)
    lift0 = time_step * freq0 * fields0[0] / sums0[0]
    own_gain = lift0 * float(total_vel)
    own_keep = 1.0 - time_step * freq0
    lax.fori_loop(1, CHUNKS - 1, first_transport, 0)
    third[0].wait_recv()
    fields_x, their_quad, freq_x = coefficient_rows(rows_of(total_theirs[...]))
    norm_x = gauss_total(their_quad, cells, z_count) * inv_total
    their_gain = time_step * freq_x * fields_x[0] / norm_x
    their_keep = 1.0 - time_step * freq_x
    quad0 = [jnp.concatenate([a, b], axis=1) for a, b in zip(own_quad, their_quad)]
    gain0 = jnp.concatenate([own_gain, their_gain], axis=1)
    keep0 = jnp.concatenate([own_keep, their_keep], axis=1)
    ahead = nodes - rows
    phi = phi_ref[...]
    m_t0 = split_dot(phi[:, :ahead], tr0[:ahead, :cells])
    lax.fori_loop(CHUNKS - 1, CHUNKS, first_transport, 0)
    qb1[me_q] = (m_t0 + split_dot(phi[:, ahead:], tr0[ahead:, :cells])) * inv_total
    fourth = in_quad(qb1, d_s, d_r)

    def second_transport(c, carry):
        part, state = wide(c)
        vx, vy, vz = local_velocity(c, both)
        state = keep0 * state - time_step * tr0[part, :] + gain0 * jnp.exp2(exponent_at(quad0, vx, vy, vz))
        fnew[part, :] = state[:, :cells]
        tr1[part, :] = transport(state, c, cells)
        return carry

    lax.fori_loop(0, CHUNKS - 1, second_transport, 0)
    zb1[me_z] = collect(fourth, qb1, QUAD)
    sixth = along_z(zb1, g_s, g_r)
    lax.fori_loop(CHUNKS - 1, CHUNKS, second_transport, 0)
    qb2[me_q] = split_dot(phi, tr1[...]) * inv_total
    fifth = in_quad(qb2, e_s, e_r)
    zb2[me_z] = collect(fifth, qb2, QUAD)
    seventh = along_z(zb2, h_s, h_r)
    mom_t0 = collect(sixth, zb1, ring)
    mom1 = [
        own_keep * mom0[r] - time_step * mom_t0[r : r + 1] + lift0 * sums0[r] for r in range(13)
    ]
    fields1, quad1, freq1 = coefficient_rows(mom1)
    sums = gauss_moments(quad1, cells, z_count)
    inv_sum = 1.0 / sums[0]
    lift = time_step * freq1 * fields1[0]
    gain1 = lift * inv_sum * float(total_vel)
    keep1 = 1.0 - time_step * freq1

    def store(c):
        part = pl.ds(pl.multiple_of(c * rows, rows), rows)
        return pltpu.make_async_copy(out_ref.at[part], out_hbm.at[part], store_s.at[c])

    def finish(c, carry):
        part = pl.ds(pl.multiple_of(c * rows, rows), rows)
        vx, vy, vz = local_velocity(c, cells)
        out_ref[part, :] = (
            keep1 * fnew[part, :] - time_step * tr1[part, :]
            + gain1 * jnp.exp2(exponent_at(quad1, vx, vy, vz))
        )
        store(c).start()
        return carry

    lax.fori_loop(0, CHUNKS, finish, 0)
    mom_t = collect(seventh, zb2, ring)
    slope = lift * inv_sum
    last = [
        keep1 * mom1[r] - time_step * mom_t[r : r + 1] + slope * sums[r] for r in range(13)
    ]
    final = macroscopic_rows(last)
    for r in range(13):
        fields_ref[r : r + 1, :] = final[r]
    for c in range(CHUNKS):
        store(c).wait()
    for c in range(PIECES):
        bulk(c).wait_send()
    for copy in metas + first + second + third + fourth + fifth + sixth + seventh:
        copy.wait_send()


def per_device_pair(distribution, normals, adjacency, send_list, block_counts):
    nodes, cells = distribution.shape
    normals = normals.transpose(1, 0, 2)
    size = lax.axis_size("vel")
    ring = size // QUAD
    f32 = jnp.float32
    dma = pltpu.SemaphoreType.DMA
    vmem = pl.BlockSpec(memory_space=pltpu.VMEM)
    anywhere = pl.BlockSpec(memory_space=pl.ANY)
    return pl.pallas_call(
        functools.partial(step_kernel, nodes * size),
        out_shape=(
            jax.ShapeDtypeStruct((nodes, cells), f32),
            jax.ShapeDtypeStruct((13, cells), f32),
        ),
        in_specs=[anywhere] + [vmem] * 3,
        out_specs=(anywhere, vmem),
        scratch_shapes=[
            pltpu.VMEM((nodes, cells), f32),
            pltpu.VMEM((nodes, cells), f32),
            dma,
            dma((CHUNKS,)),
            pltpu.VMEM((nodes, cells), f32),
            pltpu.VMEM(normals.shape, f32),
            pltpu.VMEM(adjacency.shape, jnp.int32),
            pltpu.VMEM(send_list.shape, jnp.int32),
            pltpu.VMEM((normals.shape[1], 2 * cells, 2 * cells), jnp.bfloat16),
            pltpu.VMEM((nodes, 2 * cells), f32),
            pltpu.VMEM((nodes, cells), f32),
            pltpu.VMEM((nodes, cells), f32),
            pltpu.VMEM((16, nodes), f32),
            pltpu.VMEM((QUAD, 16, cells), f32),
            pltpu.VMEM((ring, 16, cells), f32),
            pltpu.VMEM((16, cells), f32),
            pltpu.VMEM((16, cells), f32),
            pltpu.VMEM((QUAD, 16, cells), f32),
            pltpu.VMEM((ring, 16, cells), f32),
            pltpu.VMEM((QUAD, 16, cells), f32),
            pltpu.VMEM((ring, 16, cells), f32),
            dma((PIECES,)), dma((PIECES,)), dma((3,)), dma((3,)),
            dma((QUAD,)), dma((QUAD,)), dma((ring,)), dma((ring,)), dma, dma,
            dma((QUAD,)), dma((QUAD,)), dma((QUAD,)), dma((QUAD,)),
            dma((ring,)), dma((ring,)), dma((ring,)), dma((ring,)),
        ],
        compiler_params=pltpu.CompilerParams(collective_id=0, has_side_effects=True),
        name="steps",
    )(distribution, normals, adjacency, send_list)


def solution(mesh):
    placed = (
        P("vel", "space"),
        P(None, None, "space"),
        P(None, "space"),
        P("space", None, None),
        P(None, "space"),
    )
    pair = mesh.shape["space"] == 2 and mesh.shape["vel"] % QUAD == 0 and ITERS == 2
    return jax.shard_map(
        per_device_pair if pair else per_device,
        mesh=mesh,
        in_specs=placed,
        out_specs=(P("vel", "space"), P(None, "space")),
        check_vma=False,
    )
```
